32 devices in a mesh: tm: 4 (over y, x), op: 8 (over z, core).
Axes of the slice: x: 2, y: 2, z: 4, core: 2. Of those that a mesh axis runs over, the one named last changes fastest.
Arguments:
- sink_elem: bfloat16 [2, 4, 2048, 16384], P(None, 'tm', 'op'), may hold values from -6 to 6
- source_elem: bfloat16 [2, 2, 2048, 16384], P(None, None, None, 'op'), may hold values from -6 to 6
- peram: bfloat16 [2, 4, 2, 512, 512], P(None, 'tm', None, 'op'), may hold values from -4 to 4
- pair_list: int32 [16, 1], replicated, may hold values from 0 to 15
- spin_sets: int32 [16, 3], replicated, may hold values from 0 to 3
Outputs:
- correlator: float32 [2, 4, 2, 16, 1], P(None, 'tm')
The draws below stay inside these ranges and needn't reach their ends.
All inputs are finite; a program needn't handle non-finite values.
Results may differ from the reference program's by a relative error of at most 0.0041.
Values may be sent and summed in bfloat16 or wider, within the bound.
No kernel may reach another device: no remote copies, remote signals or barrier semaphores. Data moves between devices by JAX's collectives and lax.ppermute only.
A program may use at most 256 MiB of HBM per device.

```python
import jax
import jax.numpy as jnp
from jax import lax

NEV = 128
NSPIN = 4
NOP = 16
TSRC = 2
PAIRS = 1
TSNK = 4


def plant(entries, stream_key, smallest, top_value):
    longest = entries.shape.index(max(entries.shape))
    spots = []
    for shift in (0, 1):
        where = [jax.random.randint(jax.random.fold_in(stream_key, axis), (), 0, length) for axis, length in enumerate(entries.shape)]
        where[longest] = (where[longest] + shift) % entries.shape[longest]
        spots.append(tuple(where))
    return entries.at[spots[0]].set(smallest).at[spots[1]].set(top_value)


def block_levels(key, shape, cuts, low, high):
    level = 1.0
    for position, shards_of in cuts:
        draws = jax.random.uniform(jax.random.fold_in(jax.random.fold_in(key, 6), position), (shards_of,), jnp.float32, low / len(cuts), high / len(cuts))
        level = level * jnp.repeat(jnp.exp(draws), shape[position] // shards_of).reshape((-1,) + (1,) * (len(shape) - 1 - position))
    return level


def gaussian(stream_key, dims, deviation, most, shards=(), held_as=jnp.bfloat16):
    loudness = block_levels(stream_key, dims, shards, -0.22, 0.18) if shards else 1.0
    result = jax.random.normal(stream_key, dims, jnp.float32) * deviation * loudness
    return jnp.minimum(jnp.maximum(result, -most), most).astype(held_as)


def setup_inputs(seed: int = 0) -> dict:
    keys = jax.random.split(jax.random.key(seed), 6)
    return {
        "sink_elem": gaussian(keys[0], (2, TSNK, NOP * NEV, NEV * NEV), 1.0, 6.0, ((1, 4), (2, 8))),
        "source_elem": gaussian(keys[1], (2, TSRC, NOP * NEV, NEV * NEV), 1.0, 6.0, ((3, 8),)),
        "peram": gaussian(keys[2], (2, TSNK, TSRC, NSPIN * NEV, NSPIN * NEV), 0.5, 4.0, ((1, 4), (3, 8))),
        "pair_list": plant(jax.random.randint(keys[3], (NOP, PAIRS), 0, NOP), jax.random.fold_in(keys[3], 1), 0, NOP - 1).astype(jnp.int32),
        "spin_sets": plant(jax.random.randint(keys[4], (NOP, 3), 0, NSPIN), jax.random.fold_in(keys[4], 1), 0, NSPIN - 1).astype(jnp.int32),
    }


def keep_bf16(value):
    return lax.optimization_barrier(value.astype(jnp.bfloat16)).astype(jnp.float32)


def reference(sink_elem, source_elem, peram, pair_list, spin_sets):
    results = []
    for t in range(TSNK):
        phi = sink_elem[:, t].astype(jnp.float32).reshape(2, NOP, NEV * NEV, NEV)
        per_time = []
        for t0 in range(TSRC):
            blocks = peram[:, t, t0].astype(jnp.float32).reshape(2, NSPIN, NEV, NSPIN, NEV)
            blocks = jnp.transpose(blocks, (1, 3, 0, 2, 4))
            source = source_elem[:, t0].astype(jnp.float32).reshape(2, NOP, NEV, NEV * NEV)
            per_slot = []
            for p in range(PAIRS):
                other = pair_list[:, p]
                third = blocks[spin_sets[:, 2], spin_sets[other, 2]]
                second = blocks[spin_sets[:, 1], spin_sets[other, 1]]
                first = blocks[spin_sets[:, 0], spin_sets[other, 0]]

                def kmode(a, b):
                    return jnp.einsum('oxk,okb->oxb', a, b)

                x_re = kmode(phi[0], third[:, 0]) - kmode(phi[1], third[:, 1])
                x_im = kmode(phi[0], third[:, 1]) + kmode(phi[1], third[:, 0])
                x_re = keep_bf16(x_re).reshape(NOP, NEV, NEV, NEV)
                x_im = keep_bf16(x_im).reshape(NOP, NEV, NEV, NEV)

                def jmode(a, b):
                    return jnp.einsum('oijk,ojb->oibk', a, b)

                y_re = jmode(x_re, second[:, 0]) - jmode(x_im, second[:, 1])
                y_im = jmode(x_re, second[:, 1]) + jmode(x_im, second[:, 0])
                y_re = keep_bf16(y_re).reshape(NOP, NEV, NEV * NEV)
                y_im = keep_bf16(y_im).reshape(NOP, NEV, NEV * NEV)
                chosen = jnp.take(source, other, axis=1)

                def inner(a, b):
                    return jnp.einsum('oic,ojc->oij', a, b)

                m_re = inner(y_re, chosen[0]) + inner(y_im, chosen[1])
                m_im = inner(y_im, chosen[0]) - inner(y_re, chosen[1])
                c_re = jnp.sum(first[:, 0] * m_re - first[:, 1] * m_im, axis=(1, 2))
                c_im = jnp.sum(first[:, 0] * m_im + first[:, 1] * m_re, axis=(1, 2))
                per_slot.append(jnp.stack([c_re, c_im]))
            per_time.append(jnp.stack(per_slot, axis=-1))
        results.append(jnp.stack(per_time, axis=1))
    return jnp.stack(results, axis=1) * (1.0 / float(NEV ** 3))
```

```python
import functools

import jax
import jax.numpy as jnp
from jax import lax
from jax.experimental import pallas as pl
from jax.experimental.pallas import tpu as pltpu
from jax.sharding import PartitionSpec as P

AXES = ("tm", "op")
CORES = 2
CHUNK = 32
ROWS = 16


def complex_matrix(block):
    upper = jnp.concatenate([block[0], block[1]], axis=1)
    lower = jnp.concatenate([-block[1], block[0]], axis=1)
    return jnp.stack([upper, lower])


def baseline_plan(nev, nspin, nop, tsrc, pairs, sink_elem, source_elem, peram, pair_list, spin_sets):
    tau_all = lax.all_gather(peram, "op", axis=3, tiled=True)
    position = lax.axis_index("op")
    rows = sink_elem.shape[2]
    local_times = sink_elem.shape[1]
    span = min(rows, nev)
    groups = rows // span
    cols = source_elem.shape[3]

    def spin_block(local, t0, left, right):
        return lax.dynamic_slice(tau_all[:, local, t0], (0, left * nev, right * nev), (2, nev, nev))

    def sink_side(local, t0, p):
        pieces = []
        for group in range(groups):
            op_now = (position * rows + group * span) // nev
            mine = spin_sets[op_now]
            theirs = spin_sets[pair_list[op_now, p]]
            third = complex_matrix(spin_block(local, t0, mine[2], theirs[2]))
            second = complex_matrix(spin_block(local, t0, mine[1], theirs[1]))
            phi = sink_elem[:, local, group * span : (group + 1) * span].reshape(2, span * nev, nev)
            x_both = jnp.einsum("cxk,ckb->xb", phi, third, preferred_element_type=jnp.float32)
            x_both = x_both.astype(jnp.bfloat16).reshape(span, nev, 2, nev)
            y_both = jnp.einsum("ijck,cjb->ibk", x_both, second, preferred_element_type=jnp.float32)
            y_both = y_both.astype(jnp.bfloat16).reshape(span, 2, nev * nev)
            pieces.append(jnp.transpose(y_both, (1, 0, 2)))
        return jnp.concatenate(pieces, axis=1)

    partial_terms = {}
    for t0 in range(tsrc):
        combos = [(local, t0, p) for local in range(local_times) for p in range(pairs)]
        stacked = jnp.stack([sink_side(local, t0, p) for local, t0, p in combos], axis=1)
        columns = lax.all_to_all(stacked, "op", split_axis=3, concat_axis=2, tiled=True)
        for index, combo in enumerate(combos):
            other = pair_list[:, combo[2]]
            source = source_elem[:, t0].reshape(2, nop, nev, cols)
            chosen = jnp.take(source, other, axis=1)
            tiles = columns[:, index].reshape(2, nop, nev, cols)

            def inner(a, b):
                return jnp.einsum("oic,ojc->oij", a, b, preferred_element_type=jnp.float32)

            m_re = inner(tiles[0], chosen[0]) + inner(tiles[1], chosen[1])
            m_im = inner(tiles[1], chosen[0]) - inner(tiles[0], chosen[1])
            blocks = tau_all[:, combo[0], t0].reshape(2, nspin, nev, nspin, nev)
            blocks = jnp.transpose(blocks, (1, 3, 0, 2, 4))
            first = blocks[spin_sets[:, 0], spin_sets[other, 0]].astype(jnp.float32)
            c_re = jnp.sum(first[:, 0] * m_re - first[:, 1] * m_im, axis=(1, 2))
            c_im = jnp.sum(first[:, 0] * m_im + first[:, 1] * m_re, axis=(1, 2))
            partial_terms[combo] = jnp.stack([c_re, c_im])
    per_local = []
    for local in range(local_times):
        per_time = [
            jnp.stack([partial_terms[local, t0, p] for p in range(pairs)], axis=-1) for t0 in range(tsrc)
        ]
        per_local.append(jnp.stack(per_time, axis=1))
    totals = lax.psum(jnp.stack(per_local, axis=1), "op")
    return totals * (1.0 / float(nev**3))


def mode_kernel(nev, tsrc, rows, group, phi_ref, third_ref, second_ref, y_ref, xs, ys):
    def x_step(step, carry):
        lines = []
        for inner in range(group):
            at = pl.multiple_of((step * group + inner) * nev, nev)
            lines.append(jnp.concatenate([phi_ref[0, :, pl.ds(at, nev)], phi_ref[1, :, pl.ds(at, nev)]], axis=1))
        lhs = jnp.concatenate(lines, axis=0)
        out = jnp.dot(lhs, third_ref[...], preferred_element_type=jnp.float32)
        start = pl.multiple_of(step * group * rows, group * rows)
        for n in range(2 * tsrc):
            xs[n, pl.ds(start, group * rows), :] = out[:, n * nev : (n + 1) * nev]
        return carry

    lax.fori_loop(0, nev // group, x_step, 0)

    for t0 in range(tsrc):
        for pair in range(0, rows, 2):
            sides = []
            for i in (pair, pair + 1):
                halves = [xs[2 * t0 + n, pl.ds(i, nev, stride=rows), :].astype(jnp.bfloat16) for n in range(2)]
                sides.append(jnp.concatenate(halves, axis=0))
            out = jnp.dot(second_ref[t0], jnp.concatenate(sides, axis=1), preferred_element_type=jnp.float32)
            for which, i in enumerate((pair, pair + 1)):
                for n in range(2):
                    ys[n, pl.ds(i, nev, stride=rows), :] = out[n * nev : (n + 1) * nev, which * nev : (which + 1) * nev]

        def y_step(step, carry):
            for inner in range(group):
                at = pl.multiple_of((step * group + inner) * nev, nev)
                line = pl.multiple_of((step * group + inner) * rows, rows)
                for n in range(2):
                    y_ref[t0, n, :, pl.ds(at, nev)] = ys[n, pl.ds(line, rows), :].astype(jnp.bfloat16)
            return carry

        lax.fori_loop(0, nev // group, y_step, 0)


def modes(nev, tsrc, phi, third, second):
    lines, width = phi.shape[1:]
    return pl.pallas_call(
        functools.partial(mode_kernel, nev, tsrc, ROWS, 16),
        out_shape=jax.ShapeDtypeStruct((tsrc, 2, lines, width), jnp.bfloat16),
        grid=(lines // ROWS,),
        in_specs=[
            pl.BlockSpec((2, ROWS, width), lambda s: (0, s, 0)),
            pl.BlockSpec(third.shape, lambda s: (0, 0)),
            pl.BlockSpec(second.shape, lambda s: (0, 0, 0)),
        ],
        out_specs=pl.BlockSpec((tsrc, 2, ROWS, width), lambda s: (0, 0, s, 0)),
        scratch_shapes=[
            pltpu.VMEM((2 * tsrc, nev * ROWS, nev), jnp.float32),
            pltpu.VMEM((2, nev * ROWS, nev), jnp.float32),
        ],
        compiler_params=pltpu.CompilerParams(vmem_limit_bytes=48 << 20),
        name="modes",
    )(phi, third, second)


def inner_kernel(tsrc, slots, chunks, blocks, steps, where_ref, *refs):
    ys = refs[: blocks * slots * chunks]
    sources = refs[blocks * slots * chunks : blocks * (slots * chunks + 1)]
    out_ref = refs[-1]

    @pl.when(pl.program_id(0) == 0)
    def _():
        out_ref[...] = jnp.zeros_like(out_ref)

    for t0 in range(tsrc):
        total = None
        for block in range(blocks):
            mine = ys[block * slots * chunks : (block + 1) * slots * chunks]
            lhs = jnp.concatenate(
                [
                    mine[slot * chunks + chunk][t0, n]
                    for slot in range(slots)
                    for n in range(2)
                    for chunk in range(chunks)
                ],
                axis=0,
            )
            rhs = jnp.concatenate([sources[block][n, t0] for n in range(2)], axis=0)
            part = lax.dot_general(lhs, rhs, (((1,), (1,)), ((), ())), preferred_element_type=jnp.float32)
            total = part if total is None else total + part
        out_ref[t0] += total


def inner_products(nev, tsrc, ys, sources, where, parts):
    slots, chunks, blocks = len(ys), len(ys[0]), len(sources)
    cols = sources[0].shape[3]
    width = cols // parts
    lines = ys[0][0].shape[2]

    def y_spec(block):
        return pl.BlockSpec((tsrc, 2, lines, width), lambda s, w: (0, 0, 0, w[block] * parts + s))

    flat = [piece for slot in ys for piece in slot]
    specs = [y_spec(block) for block in range(blocks) for _ in flat]
    specs += [pl.BlockSpec((2, tsrc, nev, width), lambda s, w: (0, 0, 0, s)) for _ in sources]
    return pl.pallas_call(
        functools.partial(inner_kernel, tsrc, slots, chunks, blocks, parts),
        out_shape=jax.ShapeDtypeStruct((tsrc, slots * 2 * nev, 2 * nev), jnp.float32),
        grid_spec=pltpu.PrefetchScalarGridSpec(
            num_scalar_prefetch=1,
            grid=(parts,),
            in_specs=specs,
            out_specs=pl.BlockSpec((tsrc, slots * 2 * nev, 2 * nev), lambda s, w: (0, 0, 0)),
        ),
        compiler_params=pltpu.CompilerParams(vmem_limit_bytes=48 << 20),
        name="inner",
    )(where, *(flat * blocks), *sources)


def chip_plan(nev, nop, tsrc, times, depth, sink_elem, source_elem, peram, pair_list, spin_sets):
    held = sink_elem.shape[2] // nev
    chips = depth // CORES
    t = lax.axis_index("tm")
    d = lax.axis_index("op")
    z, core = d // CORES, d % CORES
    cols = source_elem.shape[3]

    def over(target):
        pairs = []
        for a in range(times):
            for b in range(depth):
                to, at, side = target(a, b // CORES, b % CORES)
                pairs.append((a * depth + b, to * depth + at * CORES + side))
        return pairs

    sources = []
    for r in range(chips):
        goal = (z + r) % chips
        q = pair_list[times * goal + t, 0]
        piece = lax.dynamic_slice(source_elem, (0, 0, q * nev, 0), (2, tsrc, nev, cols))
        if r:
            piece = lax.ppermute(piece, AXES, over(lambda a, b, c: (a, (b + r) % chips, c)))
        other = lax.ppermute(piece, AXES, over(lambda a, b, c: (a, b, (c + 1) % CORES)))
        sources.append((piece, other))

    tau_all = lax.all_gather(peram, "op", axis=3, tiled=True)[:, 0]
    chunks = nev // CHUNK

    def route(e):
        return over(lambda a, b, c: (c * held + (e + a) % held, b, a // held))

    first, second, third, phis = [], [], [], []
    for e in range(held):
        local = (e + t) % held
        op_now = d * held + local
        mine = spin_sets[op_now]
        theirs = spin_sets[pair_list[op_now, 0]]
        blocks = jnp.stack(
            [
                lax.dynamic_slice(tau_all, (0, 0, mine[n] * nev, theirs[n] * nev), (2, tsrc, nev, nev))
                for n in range(3)
            ]
        )
        blocks = lax.ppermute(blocks, AXES, route(e))
        first.append(blocks[0].astype(jnp.float32))
        turned = jnp.swapaxes(blocks[1], -1, -2)
        second.append(
            jnp.concatenate(
                [
                    jnp.concatenate([turned[0], -turned[1]], axis=2),
                    jnp.concatenate([turned[1], turned[0]], axis=2),
                ],
                axis=1,
            )
        )
        re, im = blocks[2][0], blocks[2][1]
        upper = jnp.concatenate([jnp.concatenate([re[n], im[n]], axis=1) for n in range(tsrc)], axis=1)
        lower = jnp.concatenate([jnp.concatenate([-im[n], re[n]], axis=1) for n in range(tsrc)], axis=1)
        third.append(jnp.concatenate([upper, lower], axis=0))

    arrived = []
    for h in range(chunks):
        row = []
        for e in range(held):
            local = (e + t) % held
            piece = lax.dynamic_slice(
                sink_elem[:, 0], (0, local * nev + h * CHUNK, 0), (2, CHUNK, sink_elem.shape[3])
            )
            if h >= 2:
                piece, _ = lax.optimization_barrier((piece, arrived[h - 2][e][0, 0, :128]))
            row.append(lax.ppermute(piece, AXES, route(e)))
        arrived.append(row)

    ys = [[modes(nev, tsrc, arrived[h][e], third[e], second[e]) for h in range(chunks)] for e in range(held)]

    m = None
    for r in range(chips):
        came = (z - r) % chips
        where = jnp.stack([came * CORES + core, came * CORES + (core + 1) % CORES]).astype(jnp.int32)
        part = inner_products(nev, tsrc, ys, sources[r], where, 4)
        m = part if m is None else m + part
    m = m.reshape(tsrc, held, 2, nev, 2, nev)
    m_re = m[:, :, 0, :, 0] + m[:, :, 1, :, 1]
    m_im = m[:, :, 1, :, 0] - m[:, :, 0, :, 1]
    f = jnp.stack(first)
    f_re, f_im = jnp.swapaxes(f[:, 0], 0, 1), jnp.swapaxes(f[:, 1], 0, 1)
    c_re = jnp.sum(f_re * m_re - f_im * m_im, axis=(2, 3))
    c_im = jnp.sum(f_re * m_im + f_im * m_re, axis=(2, 3))
    mine = jnp.stack([c_re, c_im])
    table = jnp.zeros((2, times, tsrc, nop, 1), jnp.float32)
    for e in range(held):
        when = core * held + (t - e) % held
        table = lax.dynamic_update_slice(table, mine[:, None, :, e, None, None], (0, when, 0, z * times + t, 0))
    table = lax.psum(table, AXES)
    return lax.dynamic_slice(table, (0, t, 0, 0, 0), (2, 1, tsrc, nop, 1)) * (1.0 / float(nev**3))


def solution(mesh):
    times, depth = mesh.shape["tm"], mesh.shape["op"]

    def on_device(sink_elem, source_elem, peram, pair_list, spin_sets):
        nop, pairs = pair_list.shape
        nev = source_elem.shape[2] // nop
        nspin = peram.shape[4] // nev
        tsrc = source_elem.shape[1]
        rows = sink_elem.shape[2]
        fits = (
            depth % CORES == 0
            and rows % nev == 0
            and rows // nev * CORES == times
            and sink_elem.shape[1] == 1
            and pairs == 1
            and nev % CHUNK == 0
        )
        if fits:
            return chip_plan(nev, nop, tsrc, times, depth, sink_elem, source_elem, peram, pair_list, spin_sets)
        return baseline_plan(nev, nspin, nop, tsrc, pairs, sink_elem, source_elem, peram, pair_list, spin_sets)

    in_specs = (
        P(None, "tm", "op", None),
        P(None, None, None, "op"),
        P(None, "tm", None, "op", None),
        P(),
        P(),
    )
    out_specs = P(None, "tm", None, None, None)
    return jax.shard_map(on_device, mesh=mesh, in_specs=in_specs, out_specs=out_specs, check_vma=False)
```

```python
import functools

import jax
import jax.numpy as jnp
from jax import lax
from jax.experimental import pallas as pl
from jax.experimental.pallas import tpu as pltpu
from jax.sharding import PartitionSpec as P


AXES = ("tm", "op")
CORES = 2
EIGHTHS = (2, 4, 1, 1)
ROWS = 16
PITCH = ROWS + 1


def complex_matrix(block):
    upper = jnp.concatenate([block[0], block[1]], axis=1)
    lower = jnp.concatenate([-block[1], block[0]], axis=1)
    return jnp.stack([upper, lower])


def baseline_plan(nev, nspin, nop, tsrc, pairs, sink_elem, source_elem, peram, pair_list, spin_sets):
    tau_all = lax.all_gather(peram, "op", axis=3, tiled=True)
    position = lax.axis_index("op")
    rows = sink_elem.shape[2]
    local_times = sink_elem.shape[1]
    span = min(rows, nev)
    groups = rows // span
    cols = source_elem.shape[3]

    def spin_block(local, t0, left, right):
        return lax.dynamic_slice(tau_all[:, local, t0], (0, left * nev, right * nev), (2, nev, nev))

    def sink_side(local, t0, p):
        pieces = []
        for group in range(groups):
            op_now = (position * rows + group * span) // nev
            mine = spin_sets[op_now]
            theirs = spin_sets[pair_list[op_now, p]]
            third = complex_matrix(spin_block(local, t0, mine[2], theirs[2]))
            second = complex_matrix(spin_block(local, t0, mine[1], theirs[1]))
            phi = sink_elem[:, local, group * span : (group + 1) * span].reshape(2, span * nev, nev)
            x_both = jnp.einsum("cxk,ckb->xb", phi, third, preferred_element_type=jnp.float32)
            x_both = x_both.astype(jnp.bfloat16).reshape(span, nev, 2, nev)
            y_both = jnp.einsum("ijck,cjb->ibk", x_both, second, preferred_element_type=jnp.float32)
            y_both = y_both.astype(jnp.bfloat16).reshape(span, 2, nev * nev)
            pieces.append(jnp.transpose(y_both, (1, 0, 2)))
        return jnp.concatenate(pieces, axis=1)

    partial_terms = {}
    for t0 in range(tsrc):
        combos = [(local, t0, p) for local in range(local_times) for p in range(pairs)]
        stacked = jnp.stack([sink_side(local, t0, p) for local, t0, p in combos], axis=1)
        columns = lax.all_to_all(stacked, "op", split_axis=3, concat_axis=2, tiled=True)
        for index, combo in enumerate(combos):
            other = pair_list[:, combo[2]]
            source = source_elem[:, t0].reshape(2, nop, nev, cols)
            chosen = jnp.take(source, other, axis=1)
            tiles = columns[:, index].reshape(2, nop, nev, cols)

            def inner(a, b):
                return jnp.einsum("oic,ojc->oij", a, b, preferred_element_type=jnp.float32)

            m_re = inner(tiles[0], chosen[0]) + inner(tiles[1], chosen[1])
            m_im = inner(tiles[1], chosen[0]) - inner(tiles[0], chosen[1])
            blocks = tau_all[:, combo[0], t0].reshape(2, nspin, nev, nspin, nev)
            blocks = jnp.transpose(blocks, (1, 3, 0, 2, 4))
            first = blocks[spin_sets[:, 0], spin_sets[other, 0]].astype(jnp.float32)
            c_re = jnp.sum(first[:, 0] * m_re - first[:, 1] * m_im, axis=(1, 2))
            c_im = jnp.sum(first[:, 0] * m_im + first[:, 1] * m_re, axis=(1, 2))
            partial_terms[combo] = jnp.stack([c_re, c_im])
    per_local = []
    for local in range(local_times):
        per_time = [
            jnp.stack([partial_terms[local, t0, p] for p in range(pairs)], axis=-1) for t0 in range(tsrc)
        ]
        per_local.append(jnp.stack(per_time, axis=1))
    totals = lax.psum(jnp.stack(per_local, axis=1), "op")
    return totals * (1.0 / float(nev**3))


def spin_kernel(nev, tsrc, held, chips, where_ref, pair_ref, spin_ref, mine_ref, other_ref, *outs):
    t, d = where_ref[0], where_ref[1]
    z, core = d // CORES, d % CORES
    lines = mine_ref.shape[3]
    for e in range(held):
        op_now = d * held + (e + t) % held
        q = pair_ref[op_now, 0]

        def block(n, part, t0):
            a, b = spin_ref[op_now, n], spin_ref[q, n]
            at = pl.multiple_of(b * nev, nev)
            pieces = []
            for piece in range(nev // lines):
                owner = a * (nev // lines) + piece
                r = (z - owner // CORES + chips) % chips
                same = (owner % CORES == core).astype(jnp.float32)
                near = mine_ref[r, part, t0, :, pl.ds(at, nev)].astype(jnp.float32)
                far = other_ref[r, part, t0, :, pl.ds(at, nev)].astype(jnp.float32)
                pieces.append(jnp.where(same > 0.5, near, far))
            return jnp.concatenate(pieces, axis=0)

        def put(row, left, right):
            outs[e][row : row + nev, :nev] = left.astype(jnp.bfloat16)
            outs[e][row : row + nev, nev:] = right.astype(jnp.bfloat16)

        for t0 in range(tsrc):
            re, im = block(1, 0, t0).T, block(1, 1, t0).T
            row = t0 * 2 * nev
            put(row, re, -im)
            put(row + nev, im, re)
            re, im = block(2, 0, t0), block(2, 1, t0)
            row = (tsrc + t0) * 2 * nev
            put(row, re, im)
            put(row + nev, -im, re)
            put(tsrc * 4 * nev + t0 * nev, block(0, 0, t0), block(0, 1, t0))


def spin_matrices(nev, tsrc, held, chips, where, pair_list, spin_sets, mine, other):
    shape = jax.ShapeDtypeStruct((tsrc * 5 * nev, 2 * nev), jnp.bfloat16)
    smem = pl.BlockSpec(memory_space=pltpu.SMEM)
    vmem = pl.BlockSpec(memory_space=pltpu.VMEM)
    return pl.pallas_call(
        functools.partial(spin_kernel, nev, tsrc, held, chips),
        out_shape=[shape] * held,
        in_specs=[smem, smem, smem, vmem, vmem],
        out_specs=[vmem] * held,
        compiler_params=pltpu.CompilerParams(vmem_limit_bytes=32 << 20),
        name="spins",
    )(where, pair_list, spin_sets, mine, other)


def mode_kernel(nev, tsrc, group, info_ref, own_ref, came_ref, mats_ref, y_ref, phi, xs, ys, sem):
    s, steps = pl.program_id(0), pl.num_programs(0)

    def fetch(step, slot, act):
        @pl.when(info_ref[0] == 1)
        def _():
            at = pl.multiple_of(info_ref[1] + step * ROWS, ROWS)
            act(pltpu.make_async_copy(own_ref.at[:, pl.ds(at, ROWS), :], phi.at[slot], sem.at[slot]))

        @pl.when(info_ref[0] == 0)
        def _():
            at = pl.multiple_of(step * ROWS, ROWS)
            act(pltpu.make_async_copy(came_ref.at[:, pl.ds(at, ROWS), :], phi.at[slot], sem.at[slot]))

    @pl.when(s == 0)
    def _():
        fetch(0, 0, lambda copy: copy.start())

    slot = lax.rem(s, 2)

    @pl.when(s + 1 < steps)
    def _():
        fetch(s + 1, 1 - slot, lambda copy: copy.start())

    fetch(s, slot, lambda copy: copy.wait())
    third = jnp.concatenate(
        [mats_ref[(tsrc + t0) * 2 * nev : (tsrc + t0 + 1) * 2 * nev, :] for t0 in range(tsrc)], axis=1
    )

    def x_step(step, carry):
        lines = []
        for inner in range(group):
            at = pl.multiple_of((step * group + inner) * nev, nev)
            lines.append(jnp.concatenate([phi[slot, 0, :, pl.ds(at, nev)], phi[slot, 1, :, pl.ds(at, nev)]], axis=1))
        out = jnp.dot(jnp.concatenate(lines, axis=0), third, preferred_element_type=jnp.float32)
        for n in range(2 * tsrc):
            for inner in range(group):
                xs[n, pl.ds((step * group + inner) * PITCH, ROWS), :] = out[
                    inner * ROWS : (inner + 1) * ROWS, n * nev : (n + 1) * nev
                ]
        return carry

    lax.fori_loop(0, nev // group, x_step, 0)

    for t0 in range(tsrc):
        second = mats_ref[t0 * 2 * nev : (t0 + 1) * 2 * nev, :]
        for pair in range(0, ROWS, 2):
            sides = []
            for i in (pair, pair + 1):
                halves = [xs[2 * t0 + n, pl.ds(i, nev, stride=PITCH), :].astype(jnp.bfloat16) for n in range(2)]
                sides.append(jnp.concatenate(halves, axis=0))
            out = jnp.dot(second, jnp.concatenate(sides, axis=1), preferred_element_type=jnp.float32)
            for which, i in enumerate((pair, pair + 1)):
                for n in range(2):
                    ys[n, pl.ds(i, nev, stride=PITCH), :] = out[
                        n * nev : (n + 1) * nev, which * nev : (which + 1) * nev
                    ]

        def y_step(step, carry):
            for inner in range(group):
                at = pl.multiple_of((step * group + inner) * nev, nev)
                for n in range(2):
                    y_ref[t0, n, :, pl.ds(at, nev)] = ys[n, pl.ds((step * group + inner) * PITCH, ROWS), :].astype(
                        jnp.bfloat16
                    )
            return carry

        lax.fori_loop(0, nev // group, y_step, 0)


def modes(nev, tsrc, info, own, came, mats):
    lines, width = came.shape[1:]
    return pl.pallas_call(
        functools.partial(mode_kernel, nev, tsrc, 64),
        out_shape=jax.ShapeDtypeStruct((tsrc, 2, lines, width), jnp.bfloat16),
        grid=(lines // ROWS,),
        in_specs=[
            pl.BlockSpec(memory_space=pltpu.SMEM),
            pl.BlockSpec(memory_space=pl.ANY),
            pl.BlockSpec(memory_space=pl.ANY),
            pl.BlockSpec(mats.shape, lambda s: (0, 0)),
        ],
        out_specs=pl.BlockSpec((tsrc, 2, ROWS, width), lambda s: (0, 0, s, 0)),
        scratch_shapes=[
            pltpu.VMEM((2, 2, ROWS, width), jnp.bfloat16),
            pltpu.VMEM((2 * tsrc, nev * PITCH, nev), jnp.float32),
            pltpu.VMEM((2, nev * PITCH, nev), jnp.float32),
            pltpu.SemaphoreType.DMA((2,)),
        ],
        compiler_params=pltpu.CompilerParams(vmem_limit_bytes=48 << 20),
        name="modes",
    )(info, own, came, mats)


def inner_kernel(nev, tsrc, slots, chunks, blocks, begin, where_ref, *refs):
    ys = refs[: blocks * slots * chunks]
    sources = refs[blocks * slots * chunks : blocks * (slots * chunks + 1)]
    mats = refs[blocks * (slots * chunks + 1) :][:slots]
    before_ref, out_ref, acc = refs[-3:]
    lines = acc.shape[1] // (2 * slots)

    @pl.when(pl.program_id(0) == 0)
    def _():
        acc[...] = jnp.zeros_like(acc)

    for t0 in range(tsrc):
        total = None
        for block in range(blocks):
            mine = ys[block * slots * chunks : (block + 1) * slots * chunks]
            lhs = jnp.concatenate(
                [
                    mine[slot * chunks + chunk][t0, n]
                    for slot in range(slots)
                    for n in range(2)
                    for chunk in range(chunks)
                ],
                axis=0,
            )
            rhs = jnp.concatenate([sources[block][n, t0] for n in range(2)], axis=0)
            part = lax.dot_general(lhs, rhs, (((1,), (1,)), ((), ())), preferred_element_type=jnp.float32)
            total = part if total is None else total + part
        acc[t0] += total

    @pl.when(pl.program_id(0) == pl.num_programs(0) - 1)
    def _():
        for slot in range(slots):
            for t0 in range(tsrc):
                row = tsrc * 4 * nev + t0 * nev + begin
                f_re = mats[slot][row : row + lines, :nev].astype(jnp.float32)
                f_im = mats[slot][row : row + lines, nev:].astype(jnp.float32)
                y_re = acc[t0, (2 * slot) * lines : (2 * slot + 1) * lines, :]
                y_im = acc[t0, (2 * slot + 1) * lines : (2 * slot + 2) * lines, :]
                m_re = y_re[:, :nev] + y_im[:, nev:]
                m_im = y_im[:, :nev] - y_re[:, nev:]
                at = (slot * tsrc + t0) * 2
                c_re = jnp.sum(f_re * m_re - f_im * m_im, axis=0, keepdims=True)
                c_im = jnp.sum(f_re * m_im + f_im * m_re, axis=0, keepdims=True)
                out_ref[at : at + 1, :] = before_ref[at : at + 1, :] + c_re
                out_ref[at + 1 : at + 2, :] = before_ref[at + 1 : at + 2, :] + c_im


def inner_products(nev, tsrc, ys, begin, sources, where, mats, before, parts):
    slots, chunks, blocks = len(ys), len(ys[0]), len(sources)
    width = sources[0].shape[3] // parts
    lines = sum(piece.shape[2] for piece in ys[0])

    def y_spec(block, piece):
        return pl.BlockSpec((tsrc, 2, piece.shape[2], width), lambda s, w: (0, 0, 0, w[block] * parts + s))

    flat = [piece for slot in ys for piece in slot]
    specs = [y_spec(block, piece) for block in range(blocks) for piece in flat]
    specs += [pl.BlockSpec((2, tsrc, nev, width), lambda s, w: (0, 0, 0, s)) for _ in sources]
    specs += [pl.BlockSpec(mat.shape, lambda s, w: (0, 0)) for mat in mats]
    specs += [pl.BlockSpec(before.shape, lambda s, w: (0, 0))]
    return pl.pallas_call(
        functools.partial(inner_kernel, nev, tsrc, slots, chunks, blocks, begin),
        out_shape=jax.ShapeDtypeStruct(before.shape, jnp.float32),
        grid_spec=pltpu.PrefetchScalarGridSpec(
            num_scalar_prefetch=1,
            grid=(parts,),
            in_specs=specs,
            out_specs=pl.BlockSpec(before.shape, lambda s, w: (0, 0)),
            scratch_shapes=[pltpu.VMEM((tsrc, slots * 2 * lines, 2 * nev), jnp.float32)],
        ),
        compiler_params=pltpu.CompilerParams(vmem_limit_bytes=56 << 20),
        name="inner",
    )(where, *(flat * blocks), *sources, *mats, before)


def chip_plan(nev, nop, tsrc, times, depth, sink_elem, source_elem, peram, pair_list, spin_sets):
    held = sink_elem.shape[2] // nev
    chips = depth // CORES
    t = lax.axis_index("tm")
    d = lax.axis_index("op")
    z, core = d // CORES, d % CORES
    cols = source_elem.shape[3]
    sink = sink_elem[:, 0]

    def over(target):
        pairs = []
        for a in range(times):
            for b in range(depth):
                to, at, side = target(a, b // CORES, b % CORES)
                pairs.append((a * depth + b, to * depth + at * CORES + side))
        return pairs

    def along(r):
        return over(lambda a, b, c: (a, (b + r) % chips, c))

    swap = over(lambda a, b, c: (a, b, (c + 1) % CORES))

    def move(value, pairs):
        return lax.ppermute(value, AXES, pairs)

    own = peram[:, 0]
    mine = [own] + [move(own, along(r)) for r in range(1, chips)]
    mine = jnp.stack(mine)

    def route(e):
        pairs = over(lambda a, b, c: (c * held + (e + a) % held, b, a // held))
        return [pair for pair in pairs if pair[0] != pair[1]]

    stays = [(core == t // held) & (e == 0) for e in range(held)]

    sizes = [nev // 8 * n for n in EIGHTHS]
    begins = [sum(sizes[:n]) for n in range(len(sizes))]

    def send(e, h, after):
        line = (e + t) % held * nev + begins[h]
        if after is not None:
            line, _ = lax.optimization_barrier((line, after))
        piece = lax.dynamic_slice(sink, (0, line, 0), (2, sizes[h], sink.shape[2]))
        return move(piece, route(e))

    arrived = [[send(e, 0, None) for e in range(held)]]

    sources = []
    for r in range(chips):
        q = pair_list[times * ((z + r) % chips) + t, 0]
        piece = lax.dynamic_slice(source_elem, (0, 0, q * nev, 0), (2, tsrc, nev, cols))
        if r:
            piece = move(piece, along(r))
        sources.append((piece, move(piece, swap)))

    other = move(mine, swap)
    where = jnp.stack([t, d]).astype(jnp.int32)
    made = spin_matrices(nev, tsrc, held, chips, where, pair_list, spin_sets, mine, other)
    mats = [jnp.where(stays[e], made[e], move(made[e], route(e))) for e in range(held)]
    for h in range(1, len(sizes)):
        arrived.append([send(e, h, mine) for e in range(held)])

    ys = [[] for _ in range(held)]
    for h in range(len(sizes)):
        for e in range(held):
            info = jnp.stack([stays[e].astype(jnp.int32), t % held * nev + begins[h]]).astype(jnp.int32)
            ys[e].append(modes(nev, tsrc, info, sink, arrived[h][e], mats[e]))

    half = len(sizes) // 2
    total = jnp.zeros((held * tsrc * 2, nev), jnp.float32)

    def add(total, first, last, r):
        came = (z - r) % chips
        at = jnp.stack([came * CORES + core, came * CORES + (core + 1) % CORES]).astype(jnp.int32)
        pieces = [row[first:last] for row in ys]
        return inner_products(nev, tsrc, pieces, begins[first], sources[r], at, mats, total, 2)

    for r in range(chips - 1):
        total = add(total, 0, half, r)
    for r in range(chips - 1):
        total = add(total, half, len(sizes), r)
    total = add(total, 0, len(sizes), chips - 1)

    plane = []
    for s in range(times):
        pairs = over(lambda a, b, c: (c * held + (a - s) % times // CORES, b, (a - s) % times % CORES))
        plane.append(lax.ppermute(total, AXES, pairs))
    plane = jnp.stack(plane)
    column = jnp.stack([plane] + [lax.ppermute(plane, AXES, along(r)) for r in range(1, chips)])
    values = jnp.sum(column, axis=-1).reshape(chips, times, held, tsrc, 2)
    chip_of = (z - jnp.arange(chips)) % chips
    op_of = (t % held * CORES + core + jnp.arange(times)) % times
    slot_of = (op_of - t) % held
    pick = (
        (jnp.arange(nop)[None, None, None] == (chip_of[:, None] * times + op_of[None])[:, :, None, None])
        & (jnp.arange(held)[None, None, :, None] == slot_of[None, :, None, None])
    )
    values = jnp.where(pick[..., None, None], values[:, :, :, None], 0.0)
    values = jnp.sum(values, axis=(0, 1, 2)) * (1.0 / float(nev**3))
    return jnp.transpose(values, (2, 1, 0))[:, None, :, :, None]


def solution(mesh):
    times, depth = mesh.shape["tm"], mesh.shape["op"]

    def on_device(sink_elem, source_elem, peram, pair_list, spin_sets):
        nop, pairs = pair_list.shape
        nev = source_elem.shape[2] // nop
        nspin = peram.shape[4] // nev
        tsrc = source_elem.shape[1]
        rows = sink_elem.shape[2]
        fits = (
            depth % CORES == 0
            and rows % nev == 0
            and rows // nev * CORES == times
            and sink_elem.shape[1] == 1
            and pairs == 1
            and nev % (8 * ROWS) == 0
            and nev % peram.shape[3] == 0
        )
        if fits:
            return chip_plan(nev, nop, tsrc, times, depth, sink_elem, source_elem, peram, pair_list, spin_sets)
        return baseline_plan(nev, nspin, nop, tsrc, pairs, sink_elem, source_elem, peram, pair_list, spin_sets)

    in_specs = (
        P(None, "tm", "op", None),
        P(None, None, None, "op"),
        P(None, "tm", None, "op", None),
        P(),
        P(),
    )
    out_specs = P(None, "tm", None, None, None)
    return jax.shard_map(on_device, mesh=mesh, in_specs=in_specs, out_specs=out_specs, check_vma=False)
```

```python
import functools

import jax
import jax.numpy as jnp
from jax import lax
from jax.experimental import pallas as pl
from jax.experimental.pallas import tpu as pltpu
from jax.sharding import PartitionSpec as P


AXES = ("tm", "op")
CORES = 2
EIGHTHS = (2, 2, 2, 1, 1)
ROWS = 16
STEPS = 4
PITCH = ROWS + 1


def complex_matrix(block):
    upper = jnp.concatenate([block[0], block[1]], axis=1)
    lower = jnp.concatenate([-block[1], block[0]], axis=1)
    return jnp.stack([upper, lower])


def baseline_plan(nev, nspin, nop, tsrc, pairs, sink_elem, source_elem, peram, pair_list, spin_sets):
    tau_all = lax.all_gather(peram, "op", axis=3, tiled=True)
    position = lax.axis_index("op")
    rows = sink_elem.shape[2]
    local_times = sink_elem.shape[1]
    span = min(rows, nev)
    groups = rows // span
    cols = source_elem.shape[3]

    def spin_block(local, t0, left, right):
        return lax.dynamic_slice(tau_all[:, local, t0], (0, left * nev, right * nev), (2, nev, nev))

    def sink_side(local, t0, p):
        pieces = []
        for group in range(groups):
            op_now = (position * rows + group * span) // nev
            mine = spin_sets[op_now]
            theirs = spin_sets[pair_list[op_now, p]]
            third = complex_matrix(spin_block(local, t0, mine[2], theirs[2]))
            second = complex_matrix(spin_block(local, t0, mine[1], theirs[1]))
            phi = sink_elem[:, local, group * span : (group + 1) * span].reshape(2, span * nev, nev)
            x_both = jnp.einsum("cxk,ckb->xb", phi, third, preferred_element_type=jnp.float32)
            x_both = x_both.astype(jnp.bfloat16).reshape(span, nev, 2, nev)
            y_both = jnp.einsum("ijck,cjb->ibk", x_both, second, preferred_element_type=jnp.float32)
            y_both = y_both.astype(jnp.bfloat16).reshape(span, 2, nev * nev)
            pieces.append(jnp.transpose(y_both, (1, 0, 2)))
        return jnp.concatenate(pieces, axis=1)

    partial_terms = {}
    for t0 in range(tsrc):
        combos = [(local, t0, p) for local in range(local_times) for p in range(pairs)]
        stacked = jnp.stack([sink_side(local, t0, p) for local, t0, p in combos], axis=1)
        columns = lax.all_to_all(stacked, "op", split_axis=3, concat_axis=2, tiled=True)
        for index, combo in enumerate(combos):
            other = pair_list[:, combo[2]]
            source = source_elem[:, t0].reshape(2, nop, nev, cols)
            chosen = jnp.take(source, other, axis=1)
            tiles = columns[:, index].reshape(2, nop, nev, cols)

            def inner(a, b):
                return jnp.einsum("oic,ojc->oij", a, b, preferred_element_type=jnp.float32)

            m_re = inner(tiles[0], chosen[0]) + inner(tiles[1], chosen[1])
            m_im = inner(tiles[1], chosen[0]) - inner(tiles[0], chosen[1])
            blocks = tau_all[:, combo[0], t0].reshape(2, nspin, nev, nspin, nev)
            blocks = jnp.transpose(blocks, (1, 3, 0, 2, 4))
            first = blocks[spin_sets[:, 0], spin_sets[other, 0]].astype(jnp.float32)
            c_re = jnp.sum(first[:, 0] * m_re - first[:, 1] * m_im, axis=(1, 2))
            c_im = jnp.sum(first[:, 0] * m_im + first[:, 1] * m_re, axis=(1, 2))
            partial_terms[combo] = jnp.stack([c_re, c_im])
    per_local = []
    for local in range(local_times):
        per_time = [
            jnp.stack([partial_terms[local, t0, p] for p in range(pairs)], axis=-1) for t0 in range(tsrc)
        ]
        per_local.append(jnp.stack(per_time, axis=1))
    totals = lax.psum(jnp.stack(per_local, axis=1), "op")
    return totals * (1.0 / float(nev**3))


def spin_kernel(nev, tsrc, held, chips, where_ref, pair_ref, spin_ref, mine_ref, other_ref, *outs):
    t, d = where_ref[0], where_ref[1]
    z, core = d // CORES, d % CORES
    lines = mine_ref.shape[3]
    for e in range(held):
        op_now = d * held + (e + t) % held
        q = pair_ref[op_now, 0]

        def block(n, part, t0):
            a, b = spin_ref[op_now, n], spin_ref[q, n]
            at = pl.multiple_of(b * nev, nev)
            pieces = []
            for piece in range(nev // lines):
                owner = a * (nev // lines) + piece
                r = (z - owner // CORES + chips) % chips
                same = (owner % CORES == core).astype(jnp.float32)
                near = mine_ref[r, part, t0, :, pl.ds(at, nev)].astype(jnp.float32)
                far = other_ref[r, part, t0, :, pl.ds(at, nev)].astype(jnp.float32)
                pieces.append(jnp.where(same > 0.5, near, far))
            return jnp.concatenate(pieces, axis=0)

        for n in range(3):
            for t0 in range(tsrc):
                row = (n * tsrc + t0) * nev
                for part in range(2):
                    outs[e][row : row + nev, part * nev : (part + 1) * nev] = block(n, part, t0).astype(jnp.bfloat16)


def spin_blocks(nev, tsrc, held, chips, where, pair_list, spin_sets, mine, other):
    shape = jax.ShapeDtypeStruct((tsrc * 3 * nev, 2 * nev), jnp.bfloat16)
    smem = pl.BlockSpec(memory_space=pltpu.SMEM)
    vmem = pl.BlockSpec(memory_space=pltpu.VMEM)
    return pl.pallas_call(
        functools.partial(spin_kernel, nev, tsrc, held, chips),
        out_shape=[shape] * held,
        in_specs=[smem, smem, smem, vmem, vmem],
        out_specs=[vmem] * held,
        compiler_params=pltpu.CompilerParams(vmem_limit_bytes=32 << 20),
        name="spins",
    )(where, pair_list, spin_sets, mine, other)


def matrix_kernel(nev, tsrc, held, info_ref, *refs):
    own, came, out_ref = refs[:held], refs[held : 2 * held], refs[-1]
    for e in range(held):

        def block(n, part, t0):
            row = (n * tsrc + t0) * nev
            got = came[e][row : row + nev, part * nev : (part + 1) * nev].astype(jnp.float32)
            if e == 0:
                kept = own[e][row : row + nev, part * nev : (part + 1) * nev].astype(jnp.float32)
                got = jnp.where(info_ref[0] == 1, kept, got)
            return got

        def put(row, left, right):
            out_ref[e, row : row + nev, :nev] = left.astype(jnp.bfloat16)
            out_ref[e, row : row + nev, nev:] = right.astype(jnp.bfloat16)

        for t0 in range(tsrc):
            re, im = block(1, 0, t0).T, block(1, 1, t0).T
            row = t0 * 2 * nev
            put(row, re, -im)
            put(row + nev, im, re)
            re, im = block(2, 0, t0), block(2, 1, t0)
            row = (tsrc + t0) * 2 * nev
            put(row, re, im)
            put(row + nev, -im, re)
            put(tsrc * 4 * nev + t0 * nev, block(0, 0, t0), block(0, 1, t0))


def matrices(nev, tsrc, info, own, came):
    vmem = pl.BlockSpec(memory_space=pltpu.VMEM)
    return pl.pallas_call(
        functools.partial(matrix_kernel, nev, tsrc, len(own)),
        out_shape=jax.ShapeDtypeStruct((len(own), tsrc * 5 * nev, 2 * nev), jnp.bfloat16),
        in_specs=[pl.BlockSpec(memory_space=pltpu.SMEM)] + [vmem] * (2 * len(own)),
        out_specs=vmem,
        compiler_params=pltpu.CompilerParams(vmem_limit_bytes=32 << 20),
        name="matrices",
    )(info, *own, *came)


def mode_kernel(nev, tsrc, held, group, info_ref, own_ref, *refs):
    came, (mats_ref, y_ref, phi, xs, ys, sem) = refs[:held], refs[held:]
    g, steps = pl.program_id(0), pl.num_programs(0) // held

    def fetch(at, slot, act):
        e = at // steps
        line = pl.multiple_of(lax.rem(at, steps) * ROWS, ROWS)
        stays = jnp.logical_and(e == 0, info_ref[0] == 1)

        @pl.when(stays)
        def _():
            mine = pl.multiple_of(info_ref[1] + line, ROWS)
            act(pltpu.make_async_copy(own_ref.at[:, pl.ds(mine, ROWS), :], phi.at[slot], sem.at[slot]))

        for n in range(held):

            @pl.when(jnp.logical_and(e == n, jnp.logical_not(stays)))
            def _():
                act(pltpu.make_async_copy(came[n].at[:, pl.ds(line, ROWS), :], phi.at[slot], sem.at[slot]))

    @pl.when(g == 0)
    def _():
        fetch(0, 0, lambda copy: copy.start())

    slot = lax.rem(g, 2)

    @pl.when(g + 1 < pl.num_programs(0))
    def _():
        fetch(g + 1, 1 - slot, lambda copy: copy.start())

    fetch(g, slot, lambda copy: copy.wait())
    third = jnp.concatenate(
        [mats_ref[0, (tsrc + t0) * 2 * nev : (tsrc + t0 + 1) * 2 * nev, :] for t0 in range(tsrc)], axis=1
    )

    def x_step(step, carry):
        lines = []
        for inner in range(group):
            at = pl.multiple_of((step * group + inner) * nev, nev)
            lines.append(jnp.concatenate([phi[slot, 0, :, pl.ds(at, nev)], phi[slot, 1, :, pl.ds(at, nev)]], axis=1))
        out = jnp.dot(jnp.concatenate(lines, axis=0), third, preferred_element_type=jnp.float32)
        for n in range(2 * tsrc):
            for inner in range(group):
                xs[n, pl.ds((step * group + inner) * PITCH, ROWS), :] = out[
                    inner * ROWS : (inner + 1) * ROWS, n * nev : (n + 1) * nev
                ]
        return carry

    lax.fori_loop(0, nev // group, x_step, 0)

    for t0 in range(tsrc):
        second = mats_ref[0, t0 * 2 * nev : (t0 + 1) * 2 * nev, :]
        for pair in range(0, ROWS, 2):
            sides = []
            for i in (pair, pair + 1):
                halves = [xs[2 * t0 + n, pl.ds(i, nev, stride=PITCH), :].astype(jnp.bfloat16) for n in range(2)]
                sides.append(jnp.concatenate(halves, axis=0))
            out = jnp.dot(second, jnp.concatenate(sides, axis=1), preferred_element_type=jnp.float32)
            for which, i in enumerate((pair, pair + 1)):
                for n in range(2):
                    ys[n, pl.ds(i, nev, stride=PITCH), :] = out[
                        n * nev : (n + 1) * nev, which * nev : (which + 1) * nev
                    ]

        def y_step(step, carry):
            for inner in range(group):
                at = pl.multiple_of((step * group + inner) * nev, nev)
                for n in range(2):
                    y_ref[0, t0, n, :, pl.ds(at, nev)] = ys[n, pl.ds((step * group + inner) * PITCH, ROWS), :].astype(
                        jnp.bfloat16
                    )
            return carry

        lax.fori_loop(0, nev // group, y_step, 0)


def modes(nev, tsrc, info, own, came, mats):
    held = len(came)
    lines, width = came[0].shape[1:]
    steps = lines // ROWS
    hbm = pl.BlockSpec(memory_space=pl.ANY)
    return pl.pallas_call(
        functools.partial(mode_kernel, nev, tsrc, held, 64),
        out_shape=pltpu.HBM((held, tsrc, 2, lines, width), jnp.bfloat16),
        grid=(held * steps,),
        in_specs=[pl.BlockSpec(memory_space=pltpu.SMEM), hbm]
        + [hbm] * held
        + [pl.BlockSpec((1, *mats.shape[1:]), lambda g: (g // steps, 0, 0))],
        out_specs=pl.BlockSpec((1, tsrc, 2, ROWS, width), lambda g: (g // steps, 0, 0, g % steps, 0)),
        scratch_shapes=[
            pltpu.VMEM((2, 2, ROWS, width), jnp.bfloat16),
            pltpu.VMEM((2 * tsrc, nev * PITCH, nev), jnp.float32),
            pltpu.VMEM((2, nev * PITCH, nev), jnp.float32),
            pltpu.SemaphoreType.DMA((2,)),
        ],
        compiler_params=pltpu.CompilerParams(vmem_limit_bytes=48 << 20),
        name="modes",
    )(info, own, *came, mats)


def inner_kernel(nev, tsrc, slots, counts, groups, begin, where_ref, *refs):
    refs = list(refs)

    def take(count):
        got = refs[:count]
        del refs[:count]
        return got

    ys = [[take(len(counts) - first) for _ in range(CORES)] for first in groups]
    sources = [take(CORES) for _ in groups]
    mats_ref, before_ref, out_ref, acc = refs
    lines = acc.shape[1] // (2 * slots)

    @pl.when(pl.program_id(0) == 0)
    def _():
        acc[...] = jnp.zeros_like(acc)

    for t0 in range(tsrc):
        for group, first in enumerate(groups):
            skip = sum(counts[:first])
            total = None
            for block in range(CORES):
                lhs = jnp.concatenate(
                    [piece[slot, t0, n] for slot in range(slots) for n in range(2) for piece in ys[group][block]],
                    axis=0,
                )
                rhs = jnp.concatenate([sources[group][block][n, t0] for n in range(2)], axis=0)
                part = lax.dot_general(lhs, rhs, (((1,), (1,)), ((), ())), preferred_element_type=jnp.float32)
                total = part if total is None else total + part
            if skip == 0:
                acc[t0] += total
            else:
                for part in range(2 * slots):
                    own = lines - skip
                    acc[t0, part * lines + skip : (part + 1) * lines, :] += total[part * own : (part + 1) * own]

    @pl.when(pl.program_id(0) == pl.num_programs(0) - 1)
    def _():
        for slot in range(slots):
            for t0 in range(tsrc):
                row = t0 * nev + begin
                f_re = mats_ref[slot, row : row + lines, :nev].astype(jnp.float32)
                f_im = mats_ref[slot, row : row + lines, nev:].astype(jnp.float32)
                y_re = acc[t0, (2 * slot) * lines : (2 * slot + 1) * lines, :]
                y_im = acc[t0, (2 * slot + 1) * lines : (2 * slot + 2) * lines, :]
                m_re = y_re[:, :nev] + y_im[:, nev:]
                m_im = y_im[:, :nev] - y_re[:, nev:]
                at = (slot * tsrc + t0) * 2
                c_re = jnp.sum(f_re * m_re - f_im * m_im, axis=0, keepdims=True)
                c_im = jnp.sum(f_re * m_im + f_im * m_re, axis=0, keepdims=True)
                out_ref[at : at + 1, :] = before_ref[at : at + 1, :] + c_re
                out_ref[at + 1 : at + 2, :] = before_ref[at + 1 : at + 2, :] + c_im


def inner_products(nev, tsrc, ys, begin, groups, sources, where, mats, before):
    slots = ys[0].shape[0]
    counts = [piece.shape[3] for piece in ys]
    lines = sum(counts)
    args, specs = [], []
    for group, first in enumerate(groups):
        width = sources[group][0].shape[3] // STEPS
        for block in range(CORES):
            for piece in ys[first:]:
                at = group * CORES + block
                args.append(piece)
                specs.append(
                    pl.BlockSpec(
                        (slots, tsrc, 2, piece.shape[3], width), lambda s, w, at=at: (0, 0, 0, 0, w[at] + s)
                    )
                )
    for pair in sources:
        width = pair[0].shape[3] // STEPS
        for piece in pair:
            args.append(pltpu.with_memory_space_constraint(piece, pltpu.HBM))
            specs.append(pl.BlockSpec((2, tsrc, nev, width), lambda s, w: (0, 0, 0, s)))
    args += [mats, before]
    specs.append(pl.BlockSpec((slots, tsrc * nev, 2 * nev), lambda s, w: (0, 4, 0)))
    specs.append(pl.BlockSpec(before.shape, lambda s, w: (0, 0)))
    return pl.pallas_call(
        functools.partial(inner_kernel, nev, tsrc, slots, counts, groups, begin),
        out_shape=jax.ShapeDtypeStruct(before.shape, jnp.float32),
        grid_spec=pltpu.PrefetchScalarGridSpec(
            num_scalar_prefetch=1,
            grid=(STEPS,),
            in_specs=specs,
            out_specs=pl.BlockSpec(before.shape, lambda s, w: (0, 0)),
            scratch_shapes=[pltpu.VMEM((tsrc, slots * 2 * lines, 2 * nev), jnp.float32)],
        ),
        compiler_params=pltpu.CompilerParams(vmem_limit_bytes=56 << 20),
        name="inner",
    )(where, *args)


def chip_plan(nev, nop, tsrc, times, depth, sink_elem, source_elem, peram, pair_list, spin_sets):
    held = sink_elem.shape[2] // nev
    chips = depth // CORES
    t = lax.axis_index("tm")
    d = lax.axis_index("op")
    z, core = d // CORES, d % CORES
    cols = source_elem.shape[3]
    sink = sink_elem[:, 0]

    def over(target):
        pairs = []
        for a in range(times):
            for b in range(depth):
                to, at, side = target(a, b // CORES, b % CORES)
                pairs.append((a * depth + b, to * depth + at * CORES + side))
        return pairs

    def along(r):
        return over(lambda a, b, c: (a, (b + r) % chips, c))

    swap = over(lambda a, b, c: (a, b, (c + 1) % CORES))

    def move(value, pairs):
        return lax.ppermute(value, AXES, pairs)

    own = peram[:, 0]
    mine = [own] + [move(own, along(r)) for r in range(1, chips)]
    mine = jnp.stack(mine)

    def route(e):
        pairs = over(lambda a, b, c: (c * held + (e + a) % held, b, a // held))
        return [pair for pair in pairs if pair[0] != pair[1]]

    stays = core == t // held

    sizes = [nev // 8 * n for n in EIGHTHS]
    begins = [sum(sizes[:n]) for n in range(len(sizes))]

    def send(e, h, after):
        line = (e + t) % held * nev + begins[h]
        piece = lax.dynamic_slice(after, (0, line, 0), (2, sizes[h], after.shape[2]))
        return move(piece, route(e))

    arrived = [[send(e, 0, sink) for e in range(held)]]

    sources = {}
    for name, r, part, parts in rounds(chips):
        q = pair_list[times * ((z + r) % chips) + t, 0]
        width = cols // parts
        piece = lax.dynamic_slice(source_elem, (0, 0, q * nev, part * width), (2, tsrc, nev, width))
        if r:
            piece = move(piece, along(r))
        sources[name] = (piece, move(piece, swap))

    other = move(mine, swap)
    where = jnp.stack([t, d]).astype(jnp.int32)
    made = spin_blocks(nev, tsrc, held, chips, where, pair_list, spin_sets, mine, other)
    info = jnp.stack([stays.astype(jnp.int32), t % held * nev]).astype(jnp.int32)
    mats = matrices(nev, tsrc, info, made, [move(made[e], route(e)) for e in range(held)])
    later, _ = lax.optimization_barrier((sink, mine))
    for h in range(1, len(sizes)):
        arrived.append([send(e, h, later) for e in range(held)])

    ys = []
    for h in range(len(sizes)):
        info = jnp.stack([stays.astype(jnp.int32), t % held * nev + begins[h]]).astype(jnp.int32)
        ys.append(modes(nev, tsrc, info, sink, arrived[h], mats))

    total = jnp.zeros((held * tsrc * 2, nev), jnp.float32)
    places = {}
    for name, r, part, parts in rounds(chips):
        came = (z - r) % chips
        places[name] = [
            ((came * CORES + side) * parts + part) * STEPS for side in (core, (core + 1) % CORES)
        ]
    for name, first, last, cuts, names in products(len(sizes), chips):
        total = inner_products(
            nev,
            tsrc,
            ys[first:last],
            begins[first],
            [cut - first for cut in cuts],
            [sources[n] for n in names],
            jnp.stack([at for n in names for at in places[n]]).astype(jnp.int32),
            mats,
            total,
        )

    plane = []
    for s in range(times):
        pairs = over(lambda a, b, c: (c * held + (a - s) % times // CORES, b, (a - s) % times % CORES))
        plane.append(lax.ppermute(total, AXES, pairs))
    plane = jnp.stack(plane)
    column = jnp.stack([plane] + [lax.ppermute(plane, AXES, along(r)) for r in range(1, chips)])
    values = jnp.sum(column, axis=-1).reshape(chips, times, held, tsrc, 2)
    chip_of = (z - jnp.arange(chips)) % chips
    op_of = (t % held * CORES + core + jnp.arange(times)) % times
    slot_of = (op_of - t) % held
    pick = (
        (jnp.arange(nop)[None, None, None] == (chip_of[:, None] * times + op_of[None])[:, :, None, None])
        & (jnp.arange(held)[None, None, :, None] == slot_of[None, :, None, None])
    )
    values = jnp.where(pick[..., None, None], values[:, :, :, None], 0.0)
    values = jnp.sum(values, axis=(0, 1, 2)) * (1.0 / float(nev**3))
    return jnp.transpose(values, (2, 1, 0))[:, None, :, :, None]


def rounds(chips):
    half = chips // 2
    pieces = [(f"{r}", r, 0, 1) for r in range(half)]
    return pieces + [(f"{r}{'ab'[part]}", r, part, 2) for part in range(2) for r in range(half, chips)]


def products(chunks, chips):
    names = [name for name, *_ in rounds(chips)]
    late = chips - chips // 2
    soon, then, last = names[: chips // 2], names[chips // 2 : -late], names[-late:]
    return [
        ("early", 0, 2, [0] * len(soon), soon),
        ("middle", 0, chunks - 1, [2] * len(soon) + [0] * len(then), soon + then),
        ("last", 0, chunks, [chunks - 1] * len(soon + then) + [0] * len(last), soon + then + last),
    ]


def solution(mesh):
    times, depth = mesh.shape["tm"], mesh.shape["op"]

    def on_device(sink_elem, source_elem, peram, pair_list, spin_sets):
        nop, pairs = pair_list.shape
        nev = source_elem.shape[2] // nop
        nspin = peram.shape[4] // nev
        tsrc = source_elem.shape[1]
        rows = sink_elem.shape[2]
        fits = (
            depth % CORES == 0
            and rows % nev == 0
            and rows // nev * CORES == times
            and sink_elem.shape[1] == 1
            and pairs == 1
            and nev % (8 * ROWS) == 0
            and nev % peram.shape[3] == 0
        )
        if fits:
            return chip_plan(nev, nop, tsrc, times, depth, sink_elem, source_elem, peram, pair_list, spin_sets)
        return baseline_plan(nev, nspin, nop, tsrc, pairs, sink_elem, source_elem, peram, pair_list, spin_sets)

    in_specs = (
        P(None, "tm", "op", None),
        P(None, None, None, "op"),
        P(None, "tm", None, "op", None),
        P(),
        P(),
    )
    out_specs = P(None, "tm", None, None, None)
    return jax.shard_map(on_device, mesh=mesh, in_specs=in_specs, out_specs=out_specs, check_vma=False)
```

```python
import functools

import jax
import jax.numpy as jnp
from jax import lax
from jax.experimental import pallas as pl
from jax.experimental.pallas import tpu as pltpu
from jax.sharding import PartitionSpec as P


AXES = ("tm", "op")
CORES = 2
EIGHTHS = (2, 2, 2, 1, 1)
ROWS = 16
STEPS = 4
PITCH = ROWS + 1


def complex_matrix(block):
    upper = jnp.concatenate([block[0], block[1]], axis=1)
    lower = jnp.concatenate([-block[1], block[0]], axis=1)
    return jnp.stack([upper, lower])


def baseline_plan(nev, nspin, nop, tsrc, pairs, sink_elem, source_elem, peram, pair_list, spin_sets):
    tau_all = lax.all_gather(peram, "op", axis=3, tiled=True)
    position = lax.axis_index("op")
    rows = sink_elem.shape[2]
    local_times = sink_elem.shape[1]
    span = min(rows, nev)
    groups = rows // span
    cols = source_elem.shape[3]

    def spin_block(local, t0, left, right):
        return lax.dynamic_slice(tau_all[:, local, t0], (0, left * nev, right * nev), (2, nev, nev))

    def sink_side(local, t0, p):
        pieces = []
        for group in range(groups):
            op_now = (position * rows + group * span) // nev
            mine = spin_sets[op_now]
            theirs = spin_sets[pair_list[op_now, p]]
            third = complex_matrix(spin_block(local, t0, mine[2], theirs[2]))
            second = complex_matrix(spin_block(local, t0, mine[1], theirs[1]))
            phi = sink_elem[:, local, group * span : (group + 1) * span].reshape(2, span * nev, nev)
            x_both = jnp.einsum("cxk,ckb->xb", phi, third, preferred_element_type=jnp.float32)
            x_both = x_both.astype(jnp.bfloat16).reshape(span, nev, 2, nev)
            y_both = jnp.einsum("ijck,cjb->ibk", x_both, second, preferred_element_type=jnp.float32)
            y_both = y_both.astype(jnp.bfloat16).reshape(span, 2, nev * nev)
            pieces.append(jnp.transpose(y_both, (1, 0, 2)))
        return jnp.concatenate(pieces, axis=1)

    partial_terms = {}
    for t0 in range(tsrc):
        combos = [(local, t0, p) for local in range(local_times) for p in range(pairs)]
        stacked = jnp.stack([sink_side(local, t0, p) for local, t0, p in combos], axis=1)
        columns = lax.all_to_all(stacked, "op", split_axis=3, concat_axis=2, tiled=True)
        for index, combo in enumerate(combos):
            other = pair_list[:, combo[2]]
            source = source_elem[:, t0].reshape(2, nop, nev, cols)
            chosen = jnp.take(source, other, axis=1)
            tiles = columns[:, index].reshape(2, nop, nev, cols)

            def inner(a, b):
                return jnp.einsum("oic,ojc->oij", a, b, preferred_element_type=jnp.float32)

            m_re = inner(tiles[0], chosen[0]) + inner(tiles[1], chosen[1])
            m_im = inner(tiles[1], chosen[0]) - inner(tiles[0], chosen[1])
            blocks = tau_all[:, combo[0], t0].reshape(2, nspin, nev, nspin, nev)
            blocks = jnp.transpose(blocks, (1, 3, 0, 2, 4))
            first = blocks[spin_sets[:, 0], spin_sets[other, 0]].astype(jnp.float32)
            c_re = jnp.sum(first[:, 0] * m_re - first[:, 1] * m_im, axis=(1, 2))
            c_im = jnp.sum(first[:, 0] * m_im + first[:, 1] * m_re, axis=(1, 2))
            partial_terms[combo] = jnp.stack([c_re, c_im])
    per_local = []
    for local in range(local_times):
        per_time = [
            jnp.stack([partial_terms[local, t0, p] for p in range(pairs)], axis=-1) for t0 in range(tsrc)
        ]
        per_local.append(jnp.stack(per_time, axis=1))
    totals = lax.psum(jnp.stack(per_local, axis=1), "op")
    return totals * (1.0 / float(nev**3))


def spin_kernel(nev, tsrc, held, chips, where_ref, pair_ref, spin_ref, mine_ref, other_ref, *outs):
    t, d = where_ref[0], where_ref[1]
    z, core = d // CORES, d % CORES
    lines = mine_ref.shape[3]
    for e in range(held):
        op_now = d * held + (e + t) % held
        q = pair_ref[op_now, 0]

        def block(n, part, t0):
            a, b = spin_ref[op_now, n], spin_ref[q, n]
            at = pl.multiple_of(b * nev, nev)
            pieces = []
            for piece in range(nev // lines):
                owner = a * (nev // lines) + piece
                r = (z - owner // CORES + chips) % chips
                same = (owner % CORES == core).astype(jnp.float32)
                near = mine_ref[r, part, t0, :, pl.ds(at, nev)].astype(jnp.float32)
                far = other_ref[r, part, t0, :, pl.ds(at, nev)].astype(jnp.float32)
                pieces.append(jnp.where(same > 0.5, near, far))
            return jnp.concatenate(pieces, axis=0)

        for n in range(3):
            for t0 in range(tsrc):
                row = (n * tsrc + t0) * nev
                for part in range(2):
                    outs[e][row : row + nev, part * nev : (part + 1) * nev] = block(n, part, t0).astype(jnp.bfloat16)


def spin_blocks(nev, tsrc, held, chips, where, pair_list, spin_sets, mine, other):
    shape = jax.ShapeDtypeStruct((tsrc * 3 * nev, 2 * nev), jnp.bfloat16)
    smem = pl.BlockSpec(memory_space=pltpu.SMEM)
    vmem = pl.BlockSpec(memory_space=pltpu.VMEM)
    return pl.pallas_call(
        functools.partial(spin_kernel, nev, tsrc, held, chips),
        out_shape=[shape] * held,
        in_specs=[smem, smem, smem, vmem, vmem],
        out_specs=[vmem] * held,
        compiler_params=pltpu.CompilerParams(vmem_limit_bytes=32 << 20),
        name="spins",
    )(where, pair_list, spin_sets, mine, other)


def matrix_kernel(nev, tsrc, held, info_ref, *refs):
    own, came, out_ref = refs[:held], refs[held : 2 * held], refs[-1]
    for e in range(held):

        def block(n, part, t0):
            row = (n * tsrc + t0) * nev
            got = came[e][row : row + nev, part * nev : (part + 1) * nev].astype(jnp.float32)
            if e == 0:
                kept = own[e][row : row + nev, part * nev : (part + 1) * nev].astype(jnp.float32)
                got = jnp.where(info_ref[0] == 1, kept, got)
            return got

        def put(row, left, right):
            out_ref[e, row : row + nev, :nev] = left.astype(jnp.bfloat16)
            out_ref[e, row : row + nev, nev:] = right.astype(jnp.bfloat16)

        for t0 in range(tsrc):
            re, im = block(1, 0, t0).T, block(1, 1, t0).T
            row = t0 * 2 * nev
            put(row, re, -im)
            put(row + nev, im, re)
            re, im = block(2, 0, t0), block(2, 1, t0)
            row = (tsrc + t0) * 2 * nev
            put(row, re, im)
            put(row + nev, -im, re)
            put(tsrc * 4 * nev + t0 * nev, block(0, 0, t0), block(0, 1, t0))


def matrices(nev, tsrc, info, own, came):
    vmem = pl.BlockSpec(memory_space=pltpu.VMEM)
    return pl.pallas_call(
        functools.partial(matrix_kernel, nev, tsrc, len(own)),
        out_shape=jax.ShapeDtypeStruct((len(own), tsrc * 5 * nev, 2 * nev), jnp.bfloat16),
        in_specs=[pl.BlockSpec(memory_space=pltpu.SMEM)] + [vmem] * (2 * len(own)),
        out_specs=vmem,
        compiler_params=pltpu.CompilerParams(vmem_limit_bytes=32 << 20),
        name="matrices",
    )(info, *own, *came)


def mode_kernel(nev, tsrc, held, group, info_ref, own_ref, *refs):
    came, (mats_ref, y_ref, phi, xs, ys, sem) = refs[:held], refs[held:]
    g, steps = pl.program_id(0), pl.num_programs(0) // held

    def fetch(at, slot, act):
        e = at // steps
        line = pl.multiple_of(lax.rem(at, steps) * ROWS, ROWS)
        stays = jnp.logical_and(e == 0, info_ref[0] == 1)

        @pl.when(stays)
        def _():
            mine = pl.multiple_of(info_ref[1] + line, ROWS)
            act(pltpu.make_async_copy(own_ref.at[:, pl.ds(mine, ROWS), :], phi.at[slot], sem.at[slot]))

        for n in range(held):

            @pl.when(jnp.logical_and(e == n, jnp.logical_not(stays)))
            def _():
                act(pltpu.make_async_copy(came[n].at[:, pl.ds(line, ROWS), :], phi.at[slot], sem.at[slot]))

    @pl.when(g == 0)
    def _():
        fetch(0, 0, lambda copy: copy.start())

    slot = lax.rem(g, 2)

    @pl.when(g + 1 < pl.num_programs(0))
    def _():
        fetch(g + 1, 1 - slot, lambda copy: copy.start())

    fetch(g, slot, lambda copy: copy.wait())
    third = jnp.concatenate(
        [mats_ref[0, (tsrc + t0) * 2 * nev : (tsrc + t0 + 1) * 2 * nev, :] for t0 in range(tsrc)], axis=1
    )

    def x_step(step, carry):
        lines = []
        for inner in range(group):
            at = pl.multiple_of((step * group + inner) * nev, nev)
            lines.append(jnp.concatenate([phi[slot, 0, :, pl.ds(at, nev)], phi[slot, 1, :, pl.ds(at, nev)]], axis=1))
        out = jnp.dot(jnp.concatenate(lines, axis=0), third, preferred_element_type=jnp.float32)
        for n in range(2 * tsrc):
            for inner in range(group):
                xs[n, pl.ds((step * group + inner) * PITCH, ROWS), :] = out[
                    inner * ROWS : (inner + 1) * ROWS, n * nev : (n + 1) * nev
                ]
        return carry

    lax.fori_loop(0, nev // group, x_step, 0)

    for t0 in range(tsrc):
        second = mats_ref[0, t0 * 2 * nev : (t0 + 1) * 2 * nev, :]
        for pair in range(0, ROWS, 2):
            sides = []
            for i in (pair, pair + 1):
                halves = [xs[2 * t0 + n, pl.ds(i, nev, stride=PITCH), :].astype(jnp.bfloat16) for n in range(2)]
                sides.append(jnp.concatenate(halves, axis=0))
            out = jnp.dot(second, jnp.concatenate(sides, axis=1), preferred_element_type=jnp.float32)
            for which, i in enumerate((pair, pair + 1)):
                for n in range(2):
                    ys[n, pl.ds(i, nev, stride=PITCH), :] = out[
                        n * nev : (n + 1) * nev, which * nev : (which + 1) * nev
                    ]

        def y_step(step, carry):
            for inner in range(group):
                at = pl.multiple_of((step * group + inner) * nev, nev)
                for n in range(2):
                    y_ref[0, t0, n, :, pl.ds(at, nev)] = ys[n, pl.ds((step * group + inner) * PITCH, ROWS), :].astype(
                        jnp.bfloat16
                    )
            return carry

        lax.fori_loop(0, nev // group, y_step, 0)


def modes(nev, tsrc, info, own, came, mats):
    held = len(came)
    lines, width = came[0].shape[1:]
    steps = lines // ROWS
    hbm = pl.BlockSpec(memory_space=pl.ANY)
    return pl.pallas_call(
        functools.partial(mode_kernel, nev, tsrc, held, 64),
        out_shape=pltpu.HBM((held, tsrc, 2, lines, width), jnp.bfloat16),
        grid=(held * steps,),
        in_specs=[pl.BlockSpec(memory_space=pltpu.SMEM), hbm]
        + [hbm] * held
        + [pl.BlockSpec((1, *mats.shape[1:]), lambda g: (g // steps, 0, 0))],
        out_specs=pl.BlockSpec((1, tsrc, 2, ROWS, width), lambda g: (g // steps, 0, 0, g % steps, 0)),
        scratch_shapes=[
            pltpu.VMEM((2, 2, ROWS, width), jnp.bfloat16),
            pltpu.VMEM((2 * tsrc, nev * PITCH, nev), jnp.float32),
            pltpu.VMEM((2, nev * PITCH, nev), jnp.float32),
            pltpu.SemaphoreType.DMA((2,)),
        ],
        compiler_params=pltpu.CompilerParams(vmem_limit_bytes=48 << 20),
        name="modes",
    )(info, own, *came, mats)


def inner_kernel(nev, tsrc, slots, counts, groups, begin, where_ref, *refs):
    refs = list(refs)

    def take(count):
        got = refs[:count]
        del refs[:count]
        return got

    ys = [[take(len(counts) - first) for _ in range(CORES)] for first in groups]
    sources = [take(CORES) for _ in groups]
    mats_ref, before_ref, out_ref, acc = refs
    lines = acc.shape[1] // (2 * slots)

    @pl.when(pl.program_id(0) == 0)
    def _():
        acc[...] = jnp.zeros_like(acc)

    for t0 in range(tsrc):
        for group, first in enumerate(groups):
            skip = sum(counts[:first])
            total = None
            for block in range(CORES):
                lhs = jnp.concatenate(
                    [piece[slot, t0, n] for slot in range(slots) for n in range(2) for piece in ys[group][block]],
                    axis=0,
                )
                rhs = jnp.concatenate([sources[group][block][n, t0] for n in range(2)], axis=0)
                part = lax.dot_general(lhs, rhs, (((1,), (1,)), ((), ())), preferred_element_type=jnp.float32)
                total = part if total is None else total + part
            if skip == 0:
                acc[t0] += total
            else:
                for part in range(2 * slots):
                    own = lines - skip
                    acc[t0, part * lines + skip : (part + 1) * lines, :] += total[part * own : (part + 1) * own]

    @pl.when(pl.program_id(0) == pl.num_programs(0) - 1)
    def _():
        for slot in range(slots):
            for t0 in range(tsrc):
                row = t0 * nev + begin
                f_re = mats_ref[slot, row : row + lines, :nev].astype(jnp.float32)
                f_im = mats_ref[slot, row : row + lines, nev:].astype(jnp.float32)
                y_re = acc[t0, (2 * slot) * lines : (2 * slot + 1) * lines, :]
                y_im = acc[t0, (2 * slot + 1) * lines : (2 * slot + 2) * lines, :]
                m_re = y_re[:, :nev] + y_im[:, nev:]
                m_im = y_im[:, :nev] - y_re[:, nev:]
                at = (slot * tsrc + t0) * 2
                c_re = jnp.sum(f_re * m_re - f_im * m_im, axis=0, keepdims=True)
                c_im = jnp.sum(f_re * m_im + f_im * m_re, axis=0, keepdims=True)
                out_ref[at : at + 1, :] = before_ref[at : at + 1, :] + c_re
                out_ref[at + 1 : at + 2, :] = before_ref[at + 1 : at + 2, :] + c_im


def inner_products(nev, tsrc, ys, begin, groups, sources, where, mats, before):
    slots = ys[0].shape[0]
    counts = [piece.shape[3] for piece in ys]
    lines = sum(counts)
    args, specs = [], []
    for group, first in enumerate(groups):
        width = sources[group][0].shape[3] // STEPS
        for block in range(CORES):
            for piece in ys[first:]:
                at = group * CORES + block
                args.append(piece)
                specs.append(
                    pl.BlockSpec(
                        (slots, tsrc, 2, piece.shape[3], width), lambda s, w, at=at: (0, 0, 0, 0, w[at] + s)
                    )
                )
    for pair in sources:
        width = pair[0].shape[3] // STEPS
        for piece in pair:
            args.append(pltpu.with_memory_space_constraint(piece, pltpu.HBM))
            specs.append(pl.BlockSpec((2, tsrc, nev, width), lambda s, w: (0, 0, 0, s)))
    args += [mats, before]
    specs.append(pl.BlockSpec((slots, tsrc * nev, 2 * nev), lambda s, w: (0, 4, 0)))
    specs.append(pl.BlockSpec(before.shape, lambda s, w: (0, 0)))
    return pl.pallas_call(
        functools.partial(inner_kernel, nev, tsrc, slots, counts, groups, begin),
        out_shape=jax.ShapeDtypeStruct(before.shape, jnp.float32),
        grid_spec=pltpu.PrefetchScalarGridSpec(
            num_scalar_prefetch=1,
            grid=(STEPS,),
            in_specs=specs,
            out_specs=pl.BlockSpec(before.shape, lambda s, w: (0, 0)),
            scratch_shapes=[pltpu.VMEM((tsrc, slots * 2 * lines, 2 * nev), jnp.float32)],
        ),
        compiler_params=pltpu.CompilerParams(vmem_limit_bytes=56 << 20),
        name="inner",
    )(where, *args)


def chip_plan(nev, nop, tsrc, times, depth, sink_elem, source_elem, peram, pair_list, spin_sets):
    held = sink_elem.shape[2] // nev
    chips = depth // CORES
    t = lax.axis_index("tm")
    d = lax.axis_index("op")
    z, core = d // CORES, d % CORES
    cols = source_elem.shape[3]
    sink = sink_elem[:, 0]

    def over(target):
        pairs = []
        for a in range(times):
            for b in range(depth):
                to, at, side = target(a, b // CORES, b % CORES)
                pairs.append((a * depth + b, to * depth + at * CORES + side))
        return pairs

    def along(r):
        return over(lambda a, b, c: (a, (b + r) % chips, c))

    swap = over(lambda a, b, c: (a, b, (c + 1) % CORES))

    def move(value, pairs):
        return lax.ppermute(value, AXES, pairs)

    own = peram[:, 0]
    mine = [own] + [move(own, along(r)) for r in range(1, chips)]
    mine = jnp.stack(mine)

    def route(e):
        pairs = over(lambda a, b, c: (c * held + (e + a) % held, b, a // held))
        return [pair for pair in pairs if pair[0] != pair[1]]

    stays = core == t // held

    sizes = [nev // 8 * n for n in EIGHTHS]
    begins = [sum(sizes[:n]) for n in range(len(sizes))]

    def send(e, h, after):
        line = (e + t) % held * nev + begins[h]
        piece = lax.dynamic_slice(after, (0, line, 0), (2, sizes[h], after.shape[2]))
        return move(piece, route(e))

    arrived = [[send(e, 0, sink) for e in range(held)]]

    sources = {}
    for name, r, part, parts in rounds(chips):
        q = pair_list[times * ((z + r) % chips) + t, 0]
        width = cols // parts
        piece = lax.dynamic_slice(source_elem, (0, 0, q * nev, part * width), (2, tsrc, nev, width))
        if r:
            piece = move(piece, along(r))
        sources[name] = (piece, move(piece, swap))

    other = move(mine, swap)
    where = jnp.stack([t, d]).astype(jnp.int32)
    made = spin_blocks(nev, tsrc, held, chips, where, pair_list, spin_sets, mine, other)
    info = jnp.stack([stays.astype(jnp.int32), t % held * nev]).astype(jnp.int32)
    mats = matrices(nev, tsrc, info, made, [move(made[e], route(e)) for e in range(held)])
    later, _ = lax.optimization_barrier((sink, mine))
    for h in range(1, len(sizes)):
        arrived.append([send(e, h, later) for e in range(held)])

    ys = []
    for h in range(len(sizes)):
        info = jnp.stack([stays.astype(jnp.int32), t % held * nev + begins[h]]).astype(jnp.int32)
        ys.append(modes(nev, tsrc, info, sink, arrived[h], mats))

    total = jnp.zeros((held * tsrc * 2, nev), jnp.float32)
    places = {}
    for name, r, part, parts in rounds(chips):
        came = (z - r) % chips
        places[name] = [
            ((came * CORES + side) * parts + part) * STEPS for side in (core, (core + 1) % CORES)
        ]
    for name, first, last, cuts, names in products(len(sizes), chips):
        total = inner_products(
            nev,
            tsrc,
            ys[first:last],
            begins[first],
            [cut - first for cut in cuts],
            [sources[n] for n in names],
            jnp.stack([at for n in names for at in places[n]]).astype(jnp.int32),
            mats,
            total,
        )

    spread = jnp.broadcast_to(total[None], (times * depth, *total.shape))
    spread = lax.all_to_all(spread, AXES, 0, 0, tiled=True)
    values = jnp.sum(spread, axis=-1).reshape(times, chips, CORES, held, tsrc, 2)
    slot_of = (jnp.arange(times) - t) % held
    pick = (jnp.arange(held)[None, None] == slot_of[:, None, None]) & (
        jnp.arange(CORES)[None, :, None] == t // held
    )
    values = jnp.where(pick[:, None, :, :, None, None], values, 0.0)
    values = jnp.sum(values, axis=(2, 3)) * (1.0 / float(nev**3))
    values = jnp.transpose(values, (3, 2, 1, 0)).reshape(2, 1, tsrc, nop, 1)
    return values


def rounds(chips):
    half = chips // 2
    pieces = [(f"{r}", r, 0, 1) for r in range(half)]
    return pieces + [(f"{r}{'ab'[part]}", r, part, 2) for part in range(2) for r in range(half, chips)]


def products(chunks, chips):
    names = [name for name, *_ in rounds(chips)]
    late = chips - chips // 2
    soon, then, last = names[: chips // 2], names[chips // 2 : -late], names[-late:]
    return [
        ("early", 0, 2, [0] * len(soon), soon),
        ("next", 2, chunks - 2, [2] * len(soon), soon),
        ("middle", 0, chunks - 1, [chunks - 2] * len(soon) + [0] * len(then), soon + then),
        ("last", 0, chunks, [chunks - 1] * len(soon + then) + [0] * len(last), soon + then + last),
    ]


def solution(mesh):
    times, depth = mesh.shape["tm"], mesh.shape["op"]

    def on_device(sink_elem, source_elem, peram, pair_list, spin_sets):
        nop, pairs = pair_list.shape
        nev = source_elem.shape[2] // nop
        nspin = peram.shape[4] // nev
        tsrc = source_elem.shape[1]
        rows = sink_elem.shape[2]
        fits = (
            depth % CORES == 0
            and rows % nev == 0
            and rows // nev * CORES == times
            and sink_elem.shape[1] == 1
            and pairs == 1
            and nev % (8 * ROWS) == 0
            and nev % peram.shape[3] == 0
        )
        if fits:
            return chip_plan(nev, nop, tsrc, times, depth, sink_elem, source_elem, peram, pair_list, spin_sets)
        return baseline_plan(nev, nspin, nop, tsrc, pairs, sink_elem, source_elem, peram, pair_list, spin_sets)

    in_specs = (
        P(None, "tm", "op", None),
        P(None, None, None, "op"),
        P(None, "tm", None, "op", None),
        P(),
        P(),
    )
    out_specs = P(None, "tm", None, None, None)
    return jax.shard_map(on_device, mesh=mesh, in_specs=in_specs, out_specs=out_specs, check_vma=False)
```

```python
import functools

import jax
import jax.numpy as jnp
from jax import lax
from jax.experimental import pallas as pl
from jax.experimental.pallas import tpu as pltpu
from jax.sharding import PartitionSpec as P


AXES = ("tm", "op")
CORES = 2
EIGHTHS = (2, 2, 2, 1, 1)
ROWS = 16
STEPS = 4
PITCH = ROWS + 1


def complex_matrix(block):
    upper = jnp.concatenate([block[0], block[1]], axis=1)
    lower = jnp.concatenate([-block[1], block[0]], axis=1)
    return jnp.stack([upper, lower])


def baseline_plan(nev, nspin, nop, tsrc, pairs, sink_elem, source_elem, peram, pair_list, spin_sets):
    tau_all = lax.all_gather(peram, "op", axis=3, tiled=True)
    position = lax.axis_index("op")
    rows = sink_elem.shape[2]
    local_times = sink_elem.shape[1]
    span = min(rows, nev)
    groups = rows // span
    cols = source_elem.shape[3]

    def spin_block(local, t0, left, right):
        return lax.dynamic_slice(tau_all[:, local, t0], (0, left * nev, right * nev), (2, nev, nev))

    def sink_side(local, t0, p):
        pieces = []
        for group in range(groups):
            op_now = (position * rows + group * span) // nev
            mine = spin_sets[op_now]
            theirs = spin_sets[pair_list[op_now, p]]
            third = complex_matrix(spin_block(local, t0, mine[2], theirs[2]))
            second = complex_matrix(spin_block(local, t0, mine[1], theirs[1]))
            phi = sink_elem[:, local, group * span : (group + 1) * span].reshape(2, span * nev, nev)
            x_both = jnp.einsum("cxk,ckb->xb", phi, third, preferred_element_type=jnp.float32)
            x_both = x_both.astype(jnp.bfloat16).reshape(span, nev, 2, nev)
            y_both = jnp.einsum("ijck,cjb->ibk", x_both, second, preferred_element_type=jnp.float32)
            y_both = y_both.astype(jnp.bfloat16).reshape(span, 2, nev * nev)
            pieces.append(jnp.transpose(y_both, (1, 0, 2)))
        return jnp.concatenate(pieces, axis=1)

    partial_terms = {}
    for t0 in range(tsrc):
        combos = [(local, t0, p) for local in range(local_times) for p in range(pairs)]
        stacked = jnp.stack([sink_side(local, t0, p) for local, t0, p in combos], axis=1)
        columns = lax.all_to_all(stacked, "op", split_axis=3, concat_axis=2, tiled=True)
        for index, combo in enumerate(combos):
            other = pair_list[:, combo[2]]
            source = source_elem[:, t0].reshape(2, nop, nev, cols)
            chosen = jnp.take(source, other, axis=1)
            tiles = columns[:, index].reshape(2, nop, nev, cols)

            def inner(a, b):
                return jnp.einsum("oic,ojc->oij", a, b, preferred_element_type=jnp.float32)

            m_re = inner(tiles[0], chosen[0]) + inner(tiles[1], chosen[1])
            m_im = inner(tiles[1], chosen[0]) - inner(tiles[0], chosen[1])
            blocks = tau_all[:, combo[0], t0].reshape(2, nspin, nev, nspin, nev)
            blocks = jnp.transpose(blocks, (1, 3, 0, 2, 4))
            first = blocks[spin_sets[:, 0], spin_sets[other, 0]].astype(jnp.float32)
            c_re = jnp.sum(first[:, 0] * m_re - first[:, 1] * m_im, axis=(1, 2))
            c_im = jnp.sum(first[:, 0] * m_im + first[:, 1] * m_re, axis=(1, 2))
            partial_terms[combo] = jnp.stack([c_re, c_im])
    per_local = []
    for local in range(local_times):
        per_time = [
            jnp.stack([partial_terms[local, t0, p] for p in range(pairs)], axis=-1) for t0 in range(tsrc)
        ]
        per_local.append(jnp.stack(per_time, axis=1))
    totals = lax.psum(jnp.stack(per_local, axis=1), "op")
    return totals * (1.0 / float(nev**3))


def spin_kernel(nev, tsrc, held, chips, where_ref, pair_ref, spin_ref, mine_ref, other_ref, *outs):
    t, d = where_ref[0], where_ref[1]
    z, core = d // CORES, d % CORES
    lines = mine_ref.shape[3]
    for e in range(held):
        op_now = d * held + (e + t) % held
        q = pair_ref[op_now, 0]

        def block(n, part, t0):
            a, b = spin_ref[op_now, n], spin_ref[q, n]
            at = pl.multiple_of(b * nev, nev)
            pieces = []
            for piece in range(nev // lines):
                owner = a * (nev // lines) + piece
                r = (z - owner // CORES + chips) % chips
                same = (owner % CORES == core).astype(jnp.float32)
                near = mine_ref[r, part, t0, :, pl.ds(at, nev)].astype(jnp.float32)
                far = other_ref[r, part, t0, :, pl.ds(at, nev)].astype(jnp.float32)
                pieces.append(jnp.where(same > 0.5, near, far))
            return jnp.concatenate(pieces, axis=0)

        for n in range(3):
            for t0 in range(tsrc):
                row = (n * tsrc + t0) * nev
                for part in range(2):
                    outs[e][row : row + nev, part * nev : (part + 1) * nev] = block(n, part, t0).astype(jnp.bfloat16)


def spin_blocks(nev, tsrc, held, chips, where, pair_list, spin_sets, mine, other):
    shape = jax.ShapeDtypeStruct((tsrc * 3 * nev, 2 * nev), jnp.bfloat16)
    smem = pl.BlockSpec(memory_space=pltpu.SMEM)
    vmem = pl.BlockSpec(memory_space=pltpu.VMEM)
    return pl.pallas_call(
        functools.partial(spin_kernel, nev, tsrc, held, chips),
        out_shape=[shape] * held,
        in_specs=[smem, smem, smem, vmem, vmem],
        out_specs=[vmem] * held,
        compiler_params=pltpu.CompilerParams(vmem_limit_bytes=32 << 20),
        name="spins",
    )(where, pair_list, spin_sets, mine, other)


def matrix_kernel(nev, tsrc, held, info_ref, *refs):
    own, came, out_ref = refs[:held], refs[held : 2 * held], refs[-1]
    for e in range(held):

        def block(n, part, t0):
            row = (n * tsrc + t0) * nev
            got = came[e][row : row + nev, part * nev : (part + 1) * nev].astype(jnp.float32)
            if e == 0:
                kept = own[e][row : row + nev, part * nev : (part + 1) * nev].astype(jnp.float32)
                got = jnp.where(info_ref[0] == 1, kept, got)
            return got

        def put(row, left, right):
            out_ref[e, row : row + nev, :nev] = left.astype(jnp.bfloat16)
            out_ref[e, row : row + nev, nev:] = right.astype(jnp.bfloat16)

        for t0 in range(tsrc):
            re, im = block(1, 0, t0).T, block(1, 1, t0).T
            row = t0 * 2 * nev
            put(row, re, -im)
            put(row + nev, im, re)
            re, im = block(2, 0, t0), block(2, 1, t0)
            row = (tsrc + t0) * 2 * nev
            put(row, re, im)
            put(row + nev, -im, re)
            put(tsrc * 4 * nev + t0 * nev, block(0, 0, t0), block(0, 1, t0))


def matrices(nev, tsrc, info, own, came):
    vmem = pl.BlockSpec(memory_space=pltpu.VMEM)
    return pl.pallas_call(
        functools.partial(matrix_kernel, nev, tsrc, len(own)),
        out_shape=jax.ShapeDtypeStruct((len(own), tsrc * 5 * nev, 2 * nev), jnp.bfloat16),
        in_specs=[pl.BlockSpec(memory_space=pltpu.SMEM)] + [vmem] * (2 * len(own)),
        out_specs=vmem,
        compiler_params=pltpu.CompilerParams(vmem_limit_bytes=32 << 20),
        name="matrices",
    )(info, *own, *came)


def mode_kernel(nev, tsrc, held, group, info_ref, own_ref, *refs):
    came, (mats_ref, y_ref, phi, xs, ys, sem) = refs[:held], refs[held:]
    g, steps = pl.program_id(0), pl.num_programs(0) // held

    def fetch(at, slot, act):
        e = at // steps
        line = pl.multiple_of(lax.rem(at, steps) * ROWS, ROWS)
        stays = jnp.logical_and(e == 0, info_ref[0] == 1)

        @pl.when(stays)
        def _():
            mine = pl.multiple_of(info_ref[1] + line, ROWS)
            act(pltpu.make_async_copy(own_ref.at[:, pl.ds(mine, ROWS), :], phi.at[slot], sem.at[slot]))

        for n in range(held):

            @pl.when(jnp.logical_and(e == n, jnp.logical_not(stays)))
            def _():
                act(pltpu.make_async_copy(came[n].at[:, pl.ds(line, ROWS), :], phi.at[slot], sem.at[slot]))

    @pl.when(g == 0)
    def _():
        fetch(0, 0, lambda copy: copy.start())

    slot = lax.rem(g, 2)

    @pl.when(g + 1 < pl.num_programs(0))
    def _():
        fetch(g + 1, 1 - slot, lambda copy: copy.start())

    fetch(g, slot, lambda copy: copy.wait())
    third = jnp.concatenate(
        [mats_ref[0, (tsrc + t0) * 2 * nev : (tsrc + t0 + 1) * 2 * nev, :] for t0 in range(tsrc)], axis=1
    )

    def x_step(step, carry):
        lines = []
        for inner in range(group):
            at = pl.multiple_of((step * group + inner) * nev, nev)
            lines.append(jnp.concatenate([phi[slot, 0, :, pl.ds(at, nev)], phi[slot, 1, :, pl.ds(at, nev)]], axis=1))
        out = jnp.dot(jnp.concatenate(lines, axis=0), third, preferred_element_type=jnp.float32)
        for n in range(2 * tsrc):
            for inner in range(group):
                xs[n, pl.ds((step * group + inner) * PITCH, ROWS), :] = out[
                    inner * ROWS : (inner + 1) * ROWS, n * nev : (n + 1) * nev
                ]
        return carry

    lax.fori_loop(0, nev // group, x_step, 0)

    for t0 in range(tsrc):
        second = mats_ref[0, t0 * 2 * nev : (t0 + 1) * 2 * nev, :]
        for pair in range(0, ROWS, 2):
            sides = []
            for i in (pair, pair + 1):
                halves = [xs[2 * t0 + n, pl.ds(i, nev, stride=PITCH), :].astype(jnp.bfloat16) for n in range(2)]
                sides.append(jnp.concatenate(halves, axis=0))
            out = jnp.dot(second, jnp.concatenate(sides, axis=1), preferred_element_type=jnp.float32)
            for which, i in enumerate((pair, pair + 1)):
                for n in range(2):
                    ys[n, pl.ds(i, nev, stride=PITCH), :] = out[
                        n * nev : (n + 1) * nev, which * nev : (which + 1) * nev
                    ]

        def y_step(step, carry):
            for inner in range(group):
                at = pl.multiple_of((step * group + inner) * nev, nev)
                for n in range(2):
                    y_ref[0, t0, n, :, pl.ds(at, nev)] = ys[n, pl.ds((step * group + inner) * PITCH, ROWS), :].astype(
                        jnp.bfloat16
                    )
            return carry

        lax.fori_loop(0, nev // group, y_step, 0)


def modes(nev, tsrc, info, own, came, mats, room):
    held = len(came)
    lines, width = came[0].shape[1:]
    steps = lines // ROWS
    hbm = pl.BlockSpec(memory_space=pl.ANY)
    return pl.pallas_call(
        functools.partial(mode_kernel, nev, tsrc, held, 64),
        out_shape=pltpu.HBM((held, tsrc, 2, lines, width), jnp.bfloat16),
        grid=(held * steps,),
        in_specs=[pl.BlockSpec(memory_space=pltpu.SMEM), hbm]
        + [hbm] * held
        + [pl.BlockSpec((1, *mats.shape[1:]), lambda g: (g // steps, 0, 0))],
        out_specs=pl.BlockSpec((1, tsrc, 2, ROWS, width), lambda g: (g // steps, 0, 0, g % steps, 0)),
        scratch_shapes=[
            pltpu.VMEM((2, 2, ROWS, width), jnp.bfloat16),
            pltpu.VMEM((2 * tsrc, nev * PITCH, nev), jnp.float32),
            pltpu.VMEM((2, nev * PITCH, nev), jnp.float32),
            pltpu.SemaphoreType.DMA((2,)),
        ],
        compiler_params=pltpu.CompilerParams(vmem_limit_bytes=room << 20),
        name="modes",
    )(info, own, *came, mats)


def inner_kernel(nev, tsrc, slots, counts, groups, begin, final, where_ref, *refs):
    refs = list(refs)

    def take(count):
        got = refs[:count]
        del refs[:count]
        return got

    ys = [[take(len(counts) - first) for _ in range(CORES)] for first in groups]
    sources = [take(CORES) for _ in groups]
    mats_ref, before_ref, out_ref, acc = refs
    lines = acc.shape[1] // (2 * slots)

    @pl.when(pl.program_id(0) == 0)
    def _():
        acc[...] = jnp.zeros_like(acc)

    for t0 in range(tsrc):
        for group, first in enumerate(groups):
            skip = sum(counts[:first])
            total = None
            for block in range(CORES):
                lhs = jnp.concatenate(
                    [piece[slot, t0, n] for slot in range(slots) for n in range(2) for piece in ys[group][block]],
                    axis=0,
                )
                rhs = jnp.concatenate([sources[group][block][n, t0] for n in range(2)], axis=0)
                part = lax.dot_general(lhs, rhs, (((1,), (1,)), ((), ())), preferred_element_type=jnp.float32)
                total = part if total is None else total + part
            if skip == 0:
                acc[t0] += total
            else:
                for part in range(2 * slots):
                    own = lines - skip
                    acc[t0, part * lines + skip : (part + 1) * lines, :] += total[part * own : (part + 1) * own]

    @pl.when(pl.program_id(0) == pl.num_programs(0) - 1)
    def _():
        for slot in range(slots):
            for t0 in range(tsrc):
                row = t0 * nev + begin
                f_re = mats_ref[slot, row : row + lines, :nev].astype(jnp.float32)
                f_im = mats_ref[slot, row : row + lines, nev:].astype(jnp.float32)
                y_re = acc[t0, (2 * slot) * lines : (2 * slot + 1) * lines, :]
                y_im = acc[t0, (2 * slot + 1) * lines : (2 * slot + 2) * lines, :]
                m_re = y_re[:, :nev] + y_im[:, nev:]
                m_im = y_im[:, :nev] - y_re[:, nev:]
                at = (slot * tsrc + t0) * 2
                c_re = jnp.sum(f_re * m_re - f_im * m_im, axis=0, keepdims=True)
                c_im = jnp.sum(f_re * m_im + f_im * m_re, axis=0, keepdims=True)
                out_ref[at : at + 1, :] = before_ref[at : at + 1, :] + c_re
                out_ref[at + 1 : at + 2, :] = before_ref[at + 1 : at + 2, :] + c_im
        if final:
            sums = jnp.sum(out_ref[...], axis=1, keepdims=True)
            row = lax.broadcasted_iota(jnp.int32, out_ref.shape, 0)
            lane = lax.broadcasted_iota(jnp.int32, out_ref.shape, 1)
            placed = jnp.sum(jnp.where(row == lane, sums, 0.0), axis=0, keepdims=True)
            out_ref[...] = jnp.broadcast_to(placed, out_ref.shape)


def inner_products(nev, tsrc, ys, begin, groups, sources, where, mats, before, final):
    slots = ys[0].shape[0]
    counts = [piece.shape[3] for piece in ys]
    lines = sum(counts)
    args, specs = [], []
    for group, first in enumerate(groups):
        width = sources[group][0].shape[3] // STEPS
        for block in range(CORES):
            for piece in ys[first:]:
                at = group * CORES + block
                args.append(piece)
                specs.append(
                    pl.BlockSpec(
                        (slots, tsrc, 2, piece.shape[3], width), lambda s, w, at=at: (0, 0, 0, 0, w[at] + s)
                    )
                )
    for pair in sources:
        width = pair[0].shape[3] // STEPS
        for piece in pair:
            args.append(pltpu.with_memory_space_constraint(piece, pltpu.HBM))
            specs.append(pl.BlockSpec((2, tsrc, nev, width), lambda s, w: (0, 0, 0, s)))
    args += [mats, before]
    specs.append(pl.BlockSpec((slots, tsrc * nev, 2 * nev), lambda s, w: (0, 4, 0)))
    specs.append(pl.BlockSpec(before.shape, lambda s, w: (0, 0)))
    return pl.pallas_call(
        functools.partial(inner_kernel, nev, tsrc, slots, counts, groups, begin, final),
        out_shape=jax.ShapeDtypeStruct(before.shape, jnp.float32),
        grid_spec=pltpu.PrefetchScalarGridSpec(
            num_scalar_prefetch=1,
            grid=(STEPS,),
            in_specs=specs,
            out_specs=pl.BlockSpec(before.shape, lambda s, w: (0, 0)),
            scratch_shapes=[pltpu.VMEM((tsrc, slots * 2 * lines, 2 * nev), jnp.float32)],
        ),
        compiler_params=pltpu.CompilerParams(vmem_limit_bytes=56 << 20),
        name="inner",
    )(where, *args)


def chip_plan(nev, nop, tsrc, times, depth, sink_elem, source_elem, peram, pair_list, spin_sets):
    held = sink_elem.shape[2] // nev
    chips = depth // CORES
    t = lax.axis_index("tm")
    d = lax.axis_index("op")
    z, core = d // CORES, d % CORES
    cols = source_elem.shape[3]
    sink = sink_elem[:, 0]

    def over(target):
        pairs = []
        for a in range(times):
            for b in range(depth):
                to, at, side = target(a, b // CORES, b % CORES)
                pairs.append((a * depth + b, to * depth + at * CORES + side))
        return pairs

    def along(r):
        return over(lambda a, b, c: (a, (b + r) % chips, c))

    swap = over(lambda a, b, c: (a, b, (c + 1) % CORES))

    def move(value, pairs):
        return lax.ppermute(value, AXES, pairs)

    own = peram[:, 0]
    mine = [own] + [move(own, along(r)) for r in range(1, chips)]
    mine = jnp.stack(mine)

    def route(e):
        pairs = over(lambda a, b, c: (c * held + (e + a) % held, b, a // held))
        return [pair for pair in pairs if pair[0] != pair[1]]

    stays = core == t // held

    sizes = [nev // 8 * n for n in EIGHTHS]
    begins = [sum(sizes[:n]) for n in range(len(sizes))]

    def send(e, h, after):
        line = (e + t) % held * nev + begins[h]
        piece = lax.dynamic_slice(after, (0, line, 0), (2, sizes[h], after.shape[2]))
        return move(piece, route(e))

    arrived = [[send(e, 0, sink) for e in range(held)]]

    sources = {}
    for name, r, part, parts in rounds(chips):
        q = pair_list[times * ((z + r) % chips) + t, 0]
        width = cols // parts
        piece = lax.dynamic_slice(source_elem, (0, 0, q * nev, part * width), (2, tsrc, nev, width))
        if r:
            piece = move(piece, along(r))
        sources[name] = (piece, move(piece, swap))

    other = move(mine, swap)
    where = jnp.stack([t, d]).astype(jnp.int32)
    made = spin_blocks(nev, tsrc, held, chips, where, pair_list, spin_sets, mine, other)
    info = jnp.stack([stays.astype(jnp.int32), t % held * nev]).astype(jnp.int32)
    mats = matrices(nev, tsrc, info, made, [move(made[e], route(e)) for e in range(held)])
    later, _ = lax.optimization_barrier((sink, mine))
    for h in range(1, len(sizes)):
        arrived.append([send(e, h, later) for e in range(held)])

    ys = []
    for h in range(len(sizes)):
        info = jnp.stack([stays.astype(jnp.int32), t % held * nev + begins[h]]).astype(jnp.int32)
        ys.append(modes(nev, tsrc, info, sink, arrived[h], mats, 48 if h < len(sizes) - 2 else 63))

    total = jnp.zeros((held * tsrc * 2, nev), jnp.float32)
    places = {}
    for name, r, part, parts in rounds(chips):
        came = (z - r) % chips
        places[name] = [
            ((came * CORES + side) * parts + part) * STEPS for side in (core, (core + 1) % CORES)
        ]
    for name, first, last, cuts, names in products(len(sizes), chips):
        total = inner_products(
            nev,
            tsrc,
            ys[first:last],
            begins[first],
            [cut - first for cut in cuts],
            [sources[n] for n in names],
            jnp.stack([at for n in names for at in places[n]]).astype(jnp.int32),
            mats,
            total,
            name == "last",
        )

    spread = jnp.broadcast_to(total[:1][None], (times * depth, 1, nev))
    spread = lax.all_to_all(spread, AXES, 0, 0, tiled=True)
    values = spread[:, 0, : held * tsrc * 2].reshape(times, chips, CORES, held, tsrc, 2)
    slot_of = (jnp.arange(times) - t) % held
    pick = (jnp.arange(held)[None, None] == slot_of[:, None, None]) & (
        jnp.arange(CORES)[None, :, None] == t // held
    )
    values = jnp.where(pick[:, None, :, :, None, None], values, 0.0)
    values = jnp.sum(values, axis=(2, 3)) * (1.0 / float(nev**3))
    values = jnp.transpose(values, (3, 2, 1, 0)).reshape(2, 1, tsrc, nop, 1)
    return values


def rounds(chips):
    half = chips // 2
    pieces = [(f"{r}", r, 0, 1) for r in range(half)]
    return pieces + [(f"{r}{'ab'[part]}", r, part, 2) for part in range(2) for r in range(half, chips)]


def products(chunks, chips):
    names = [name for name, *_ in rounds(chips)]
    late = chips - chips // 2
    soon, then, last = names[: chips // 2], names[chips // 2 : -late], names[-late:]
    return [
        ("early", 0, 2, [0] * len(soon), soon),
        ("next", 2, chunks - 2, [2] * len(soon), soon),
        ("middle", 0, chunks - 1, [chunks - 2] * len(soon) + [0] * len(then), soon + then),
        ("last", 0, chunks, [chunks - 1] * len(soon + then) + [0] * len(last), soon + then + last),
    ]


def solution(mesh):
    times, depth = mesh.shape["tm"], mesh.shape["op"]

    def on_device(sink_elem, source_elem, peram, pair_list, spin_sets):
        nop, pairs = pair_list.shape
        nev = source_elem.shape[2] // nop
        nspin = peram.shape[4] // nev
        tsrc = source_elem.shape[1]
        rows = sink_elem.shape[2]
        fits = (
            depth % CORES == 0
            and rows % nev == 0
            and rows // nev * CORES == times
            and sink_elem.shape[1] == 1
            and pairs == 1
            and nev % (8 * ROWS) == 0
            and nev % peram.shape[3] == 0
        )
        if fits:
            return chip_plan(nev, nop, tsrc, times, depth, sink_elem, source_elem, peram, pair_list, spin_sets)
        return baseline_plan(nev, nspin, nop, tsrc, pairs, sink_elem, source_elem, peram, pair_list, spin_sets)

    in_specs = (
        P(None, "tm", "op", None),
        P(None, None, None, "op"),
        P(None, "tm", None, "op", None),
        P(),
        P(),
    )
    out_specs = P(None, "tm", None, None, None)
    return jax.shard_map(on_device, mesh=mesh, in_specs=in_specs, out_specs=out_specs, check_vma=False)
```

```python
import functools

import jax
import jax.numpy as jnp
from jax import lax
from jax.experimental import pallas as pl
from jax.experimental.pallas import tpu as pltpu
from jax.sharding import PartitionSpec as P


AXES = ("tm", "op")
CORES = 2
EIGHTHS = (2, 2, 2, 1, 1)
ROWS = 16
STEPS = 4
PITCH = ROWS + 1


def complex_matrix(block):
    upper = jnp.concatenate([block[0], block[1]], axis=1)
    lower = jnp.concatenate([-block[1], block[0]], axis=1)
    return jnp.stack([upper, lower])


def baseline_plan(nev, nspin, nop, tsrc, pairs, sink_elem, source_elem, peram, pair_list, spin_sets):
    tau_all = lax.all_gather(peram, "op", axis=3, tiled=True)
    position = lax.axis_index("op")
    rows = sink_elem.shape[2]
    local_times = sink_elem.shape[1]
    span = min(rows, nev)
    groups = rows // span
    cols = source_elem.shape[3]

    def spin_block(local, t0, left, right):
        return lax.dynamic_slice(tau_all[:, local, t0], (0, left * nev, right * nev), (2, nev, nev))

    def sink_side(local, t0, p):
        pieces = []
        for group in range(groups):
            op_now = (position * rows + group * span) // nev
            mine = spin_sets[op_now]
            theirs = spin_sets[pair_list[op_now, p]]
            third = complex_matrix(spin_block(local, t0, mine[2], theirs[2]))
            second = complex_matrix(spin_block(local, t0, mine[1], theirs[1]))
            phi = sink_elem[:, local, group * span : (group + 1) * span].reshape(2, span * nev, nev)
            x_both = jnp.einsum("cxk,ckb->xb", phi, third, preferred_element_type=jnp.float32)
            x_both = x_both.astype(jnp.bfloat16).reshape(span, nev, 2, nev)
            y_both = jnp.einsum("ijck,cjb->ibk", x_both, second, preferred_element_type=jnp.float32)
            y_both = y_both.astype(jnp.bfloat16).reshape(span, 2, nev * nev)
            pieces.append(jnp.transpose(y_both, (1, 0, 2)))
        return jnp.concatenate(pieces, axis=1)

    partial_terms = {}
    for t0 in range(tsrc):
        combos = [(local, t0, p) for local in range(local_times) for p in range(pairs)]
        stacked = jnp.stack([sink_side(local, t0, p) for local, t0, p in combos], axis=1)
        columns = lax.all_to_all(stacked, "op", split_axis=3, concat_axis=2, tiled=True)
        for index, combo in enumerate(combos):
            other = pair_list[:, combo[2]]
            source = source_elem[:, t0].reshape(2, nop, nev, cols)
            chosen = jnp.take(source, other, axis=1)
            tiles = columns[:, index].reshape(2, nop, nev, cols)

            def inner(a, b):
                return jnp.einsum("oic,ojc->oij", a, b, preferred_element_type=jnp.float32)

            m_re = inner(tiles[0], chosen[0]) + inner(tiles[1], chosen[1])
            m_im = inner(tiles[1], chosen[0]) - inner(tiles[0], chosen[1])
            blocks = tau_all[:, combo[0], t0].reshape(2, nspin, nev, nspin, nev)
            blocks = jnp.transpose(blocks, (1, 3, 0, 2, 4))
            first = blocks[spin_sets[:, 0], spin_sets[other, 0]].astype(jnp.float32)
            c_re = jnp.sum(first[:, 0] * m_re - first[:, 1] * m_im, axis=(1, 2))
            c_im = jnp.sum(first[:, 0] * m_im + first[:, 1] * m_re, axis=(1, 2))
            partial_terms[combo] = jnp.stack([c_re, c_im])
    per_local = []
    for local in range(local_times):
        per_time = [
            jnp.stack([partial_terms[local, t0, p] for p in range(pairs)], axis=-1) for t0 in range(tsrc)
        ]
        per_local.append(jnp.stack(per_time, axis=1))
    totals = lax.psum(jnp.stack(per_local, axis=1), "op")
    return totals * (1.0 / float(nev**3))


def spin_kernel(nev, tsrc, held, chips, where_ref, pair_ref, spin_ref, mine_ref, other_ref, *outs):
    t, d = where_ref[0], where_ref[1]
    z, core = d // CORES, d % CORES
    lines = mine_ref.shape[3]
    for e in range(held):
        op_now = d * held + (e + t) % held
        q = pair_ref[op_now, 0]

        def block(n, part, t0):
            a, b = spin_ref[op_now, n], spin_ref[q, n]
            at = pl.multiple_of(b * nev, nev)
            pieces = []
            for piece in range(nev // lines):
                owner = a * (nev // lines) + piece
                r = (z - owner // CORES + chips) % chips
                same = (owner % CORES == core).astype(jnp.float32)
                near = mine_ref[r, part, t0, :, pl.ds(at, nev)].astype(jnp.float32)
                far = other_ref[r, part, t0, :, pl.ds(at, nev)].astype(jnp.float32)
                pieces.append(jnp.where(same > 0.5, near, far))
            return jnp.concatenate(pieces, axis=0)

        for n in range(3):
            for t0 in range(tsrc):
                row = (n * tsrc + t0) * nev
                for part in range(2):
                    outs[e][row : row + nev, part * nev : (part + 1) * nev] = block(n, part, t0).astype(jnp.bfloat16)


def spin_blocks(nev, tsrc, held, chips, where, pair_list, spin_sets, mine, other):
    shape = jax.ShapeDtypeStruct((tsrc * 3 * nev, 2 * nev), jnp.bfloat16)
    smem = pl.BlockSpec(memory_space=pltpu.SMEM)
    vmem = pl.BlockSpec(memory_space=pltpu.VMEM)
    return pl.pallas_call(
        functools.partial(spin_kernel, nev, tsrc, held, chips),
        out_shape=[shape] * held,
        in_specs=[smem, smem, smem, vmem, vmem],
        out_specs=[vmem] * held,
        compiler_params=pltpu.CompilerParams(vmem_limit_bytes=32 << 20),
        name="spins",
    )(where, pair_list, spin_sets, mine, other)


def matrix_kernel(nev, tsrc, held, info_ref, *refs):
    own, came, out_ref = refs[:held], refs[held : 2 * held], refs[-1]
    for e in range(held):

        def block(n, part, t0):
            row = (n * tsrc + t0) * nev
            got = came[e][row : row + nev, part * nev : (part + 1) * nev].astype(jnp.float32)
            if e == 0:
                kept = own[e][row : row + nev, part * nev : (part + 1) * nev].astype(jnp.float32)
                got = jnp.where(info_ref[0] == 1, kept, got)
            return got

        def put(row, left, right):
            out_ref[e, row : row + nev, :nev] = left.astype(jnp.bfloat16)
            out_ref[e, row : row + nev, nev:] = right.astype(jnp.bfloat16)

        for t0 in range(tsrc):
            re, im = block(1, 0, t0).T, block(1, 1, t0).T
            row = t0 * 2 * nev
            put(row, re, -im)
            put(row + nev, im, re)
            re, im = block(2, 0, t0), block(2, 1, t0)
            row = (tsrc + t0) * 2 * nev
            put(row, re, im)
            put(row + nev, -im, re)
            put(tsrc * 4 * nev + t0 * nev, block(0, 0, t0), block(0, 1, t0))


def matrices(nev, tsrc, info, own, came):
    vmem = pl.BlockSpec(memory_space=pltpu.VMEM)
    return pl.pallas_call(
        functools.partial(matrix_kernel, nev, tsrc, len(own)),
        out_shape=jax.ShapeDtypeStruct((len(own), tsrc * 5 * nev, 2 * nev), jnp.bfloat16),
        in_specs=[pl.BlockSpec(memory_space=pltpu.SMEM)] + [vmem] * (2 * len(own)),
        out_specs=vmem,
        compiler_params=pltpu.CompilerParams(vmem_limit_bytes=32 << 20),
        name="matrices",
    )(info, *own, *came)


def mode_kernel(nev, tsrc, held, group, info_ref, own_ref, *refs):
    came, (mats_ref, y_ref, phi, xs, ys, sem) = refs[:held], refs[held:]
    g, steps = pl.program_id(0), pl.num_programs(0) // held

    def fetch(at, slot, act):
        e = at // steps
        line = pl.multiple_of(lax.rem(at, steps) * ROWS, ROWS)
        stays = jnp.logical_and(e == 0, info_ref[0] == 1)

        @pl.when(stays)
        def _():
            mine = pl.multiple_of(info_ref[1] + line, ROWS)
            act(pltpu.make_async_copy(own_ref.at[:, pl.ds(mine, ROWS), :], phi.at[slot], sem.at[slot]))

        for n in range(held):

            @pl.when(jnp.logical_and(e == n, jnp.logical_not(stays)))
            def _():
                act(pltpu.make_async_copy(came[n].at[:, pl.ds(line, ROWS), :], phi.at[slot], sem.at[slot]))

    @pl.when(g == 0)
    def _():
        fetch(0, 0, lambda copy: copy.start())

    slot = lax.rem(g, 2)

    @pl.when(g + 1 < pl.num_programs(0))
    def _():
        fetch(g + 1, 1 - slot, lambda copy: copy.start())

    fetch(g, slot, lambda copy: copy.wait())
    third = jnp.concatenate(
        [mats_ref[0, (tsrc + t0) * 2 * nev : (tsrc + t0 + 1) * 2 * nev, :] for t0 in range(tsrc)], axis=1
    )

    def x_step(step, carry):
        lines = []
        for inner in range(group):
            at = pl.multiple_of((step * group + inner) * nev, nev)
            lines.append(jnp.concatenate([phi[slot, 0, :, pl.ds(at, nev)], phi[slot, 1, :, pl.ds(at, nev)]], axis=1))
        out = jnp.dot(jnp.concatenate(lines, axis=0), third, preferred_element_type=jnp.float32)
        for n in range(2 * tsrc):
            for inner in range(group):
                xs[n, pl.ds((step * group + inner) * PITCH, ROWS), :] = out[
                    inner * ROWS : (inner + 1) * ROWS, n * nev : (n + 1) * nev
                ]
        return carry

    lax.fori_loop(0, nev // group, x_step, 0)

    for t0 in range(tsrc):
        second = mats_ref[0, t0 * 2 * nev : (t0 + 1) * 2 * nev, :]
        for pair in range(0, ROWS, 2):
            sides = []
            for i in (pair, pair + 1):
                halves = [xs[2 * t0 + n, pl.ds(i, nev, stride=PITCH), :].astype(jnp.bfloat16) for n in range(2)]
                sides.append(jnp.concatenate(halves, axis=0))
            out = jnp.dot(second, jnp.concatenate(sides, axis=1), preferred_element_type=jnp.float32)
            for which, i in enumerate((pair, pair + 1)):
                for n in range(2):
                    ys[n, pl.ds(i, nev, stride=PITCH), :] = out[
                        n * nev : (n + 1) * nev, which * nev : (which + 1) * nev
                    ]

        def y_step(step, carry):
            for inner in range(group):
                at = pl.multiple_of((step * group + inner) * nev, nev)
                for n in range(2):
                    y_ref[0, t0, n, :, pl.ds(at, nev)] = ys[n, pl.ds((step * group + inner) * PITCH, ROWS), :].astype(
                        jnp.bfloat16
                    )
            return carry

        lax.fori_loop(0, nev // group, y_step, 0)


def modes(nev, tsrc, info, own, came, mats, room):
    held = len(came)
    lines, width = came[0].shape[1:]
    steps = lines // ROWS
    hbm = pl.BlockSpec(memory_space=pl.ANY)
    return pl.pallas_call(
        functools.partial(mode_kernel, nev, tsrc, held, 64),
        out_shape=pltpu.HBM((held, tsrc, 2, lines, width), jnp.bfloat16),
        grid=(held * steps,),
        in_specs=[pl.BlockSpec(memory_space=pltpu.SMEM), hbm]
        + [hbm] * held
        + [pl.BlockSpec((1, tsrc * 4 * nev, 2 * nev), lambda g: (g // steps, 0, 0))],
        out_specs=pl.BlockSpec((1, tsrc, 2, ROWS, width), lambda g: (g // steps, 0, 0, g % steps, 0)),
        scratch_shapes=[
            pltpu.VMEM((2, 2, ROWS, width), jnp.bfloat16),
            pltpu.VMEM((2 * tsrc, (nev + 2) * PITCH, nev), jnp.float32),
            pltpu.VMEM((2, (nev + 2) * PITCH, nev), jnp.float32),
            pltpu.SemaphoreType.DMA((2,)),
        ],
        compiler_params=pltpu.CompilerParams(vmem_limit_bytes=room << 20),
        name="modes",
    )(info, own, *came, mats)


def inner_kernel(nev, tsrc, slots, counts, groups, begin, final, where_ref, *refs):
    refs = list(refs)

    def take(count):
        got = refs[:count]
        del refs[:count]
        return got

    ys = [[take(len(counts) - first) for _ in range(CORES)] for first in groups]
    sources = [take(CORES) for _ in groups]
    mats_ref, before_ref, out_ref, acc = refs
    lines = acc.shape[1] // (2 * slots)

    @pl.when(pl.program_id(0) == 0)
    def _():
        acc[...] = jnp.zeros_like(acc)

    for t0 in range(tsrc):
        for group, first in enumerate(groups):
            skip = sum(counts[:first])
            total = None
            for block in range(CORES):
                lhs = jnp.concatenate(
                    [piece[slot, t0, n] for slot in range(slots) for n in range(2) for piece in ys[group][block]],
                    axis=0,
                )
                rhs = jnp.concatenate([sources[group][block][n, t0] for n in range(2)], axis=0)
                part = lax.dot_general(lhs, rhs, (((1,), (1,)), ((), ())), preferred_element_type=jnp.float32)
                total = part if total is None else total + part
            if skip == 0:
                acc[t0] += total
            else:
                for part in range(2 * slots):
                    own = lines - skip
                    acc[t0, part * lines + skip : (part + 1) * lines, :] += total[part * own : (part + 1) * own]

    @pl.when(pl.program_id(0) == pl.num_programs(0) - 1)
    def _():
        for slot in range(slots):
            for t0 in range(tsrc):
                row = t0 * nev + begin
                f_re = mats_ref[slot, row : row + lines, :nev].astype(jnp.float32)
                f_im = mats_ref[slot, row : row + lines, nev:].astype(jnp.float32)
                y_re = acc[t0, (2 * slot) * lines : (2 * slot + 1) * lines, :]
                y_im = acc[t0, (2 * slot + 1) * lines : (2 * slot + 2) * lines, :]
                m_re = y_re[:, :nev] + y_im[:, nev:]
                m_im = y_im[:, :nev] - y_re[:, nev:]
                at = (slot * tsrc + t0) * 2
                c_re = jnp.sum(f_re * m_re - f_im * m_im, axis=0, keepdims=True)
                c_im = jnp.sum(f_re * m_im + f_im * m_re, axis=0, keepdims=True)
                out_ref[at : at + 1, :] = before_ref[at : at + 1, :] + c_re
                out_ref[at + 1 : at + 2, :] = before_ref[at + 1 : at + 2, :] + c_im
        if final:
            sums = jnp.sum(out_ref[...], axis=1, keepdims=True)
            row = lax.broadcasted_iota(jnp.int32, out_ref.shape, 0)
            lane = lax.broadcasted_iota(jnp.int32, out_ref.shape, 1)
            placed = jnp.sum(jnp.where(row == lane, sums, 0.0), axis=0, keepdims=True)
            out_ref[...] = jnp.broadcast_to(placed, out_ref.shape)


def inner_products(nev, tsrc, ys, begin, groups, sources, where, mats, before, final):
    slots = ys[0].shape[0]
    counts = [piece.shape[3] for piece in ys]
    lines = sum(counts)
    args, specs = [], []
    for group, first in enumerate(groups):
        width = sources[group][0].shape[3] // STEPS
        for block in range(CORES):
            for piece in ys[first:]:
                at = group * CORES + block
                args.append(piece)
                specs.append(
                    pl.BlockSpec(
                        (slots, tsrc, 2, piece.shape[3], width), lambda s, w, at=at: (0, 0, 0, 0, w[at] + s)
                    )
                )
    for pair in sources:
        width = pair[0].shape[3] // STEPS
        for piece in pair:
            args.append(pltpu.with_memory_space_constraint(piece, pltpu.HBM))
            specs.append(pl.BlockSpec((2, tsrc, nev, width), lambda s, w: (0, 0, 0, s)))
    args += [mats, before]
    specs.append(pl.BlockSpec((slots, tsrc * nev, 2 * nev), lambda s, w: (0, 4, 0)))
    specs.append(pl.BlockSpec(before.shape, lambda s, w: (0, 0)))
    return pl.pallas_call(
        functools.partial(inner_kernel, nev, tsrc, slots, counts, groups, begin, final),
        out_shape=jax.ShapeDtypeStruct(before.shape, jnp.float32),
        grid_spec=pltpu.PrefetchScalarGridSpec(
            num_scalar_prefetch=1,
            grid=(STEPS,),
            in_specs=specs,
            out_specs=pl.BlockSpec(before.shape, lambda s, w: (0, 0)),
            scratch_shapes=[pltpu.VMEM((tsrc, slots * 2 * lines, 2 * nev), jnp.float32)],
        ),
        compiler_params=pltpu.CompilerParams(vmem_limit_bytes=56 << 20),
        name="inner",
    )(where, *args)


def chip_plan(nev, nop, tsrc, times, depth, sink_elem, source_elem, peram, pair_list, spin_sets):
    held = sink_elem.shape[2] // nev
    chips = depth // CORES
    t = lax.axis_index("tm")
    d = lax.axis_index("op")
    z, core = d // CORES, d % CORES
    cols = source_elem.shape[3]
    sink = sink_elem[:, 0]

    def over(target):
        pairs = []
        for a in range(times):
            for b in range(depth):
                to, at, side = target(a, b // CORES, b % CORES)
                pairs.append((a * depth + b, to * depth + at * CORES + side))
        return pairs

    def along(r):
        return over(lambda a, b, c: (a, (b + r) % chips, c))

    swap = over(lambda a, b, c: (a, b, (c + 1) % CORES))

    def move(value, pairs):
        return lax.ppermute(value, AXES, pairs)

    own = peram[:, 0]
    mine = [own] + [move(own, along(r)) for r in range(1, chips)]
    mine = jnp.stack(mine)

    def route(e):
        pairs = over(lambda a, b, c: (c * held + (e + a) % held, b, a // held))
        return [pair for pair in pairs if pair[0] != pair[1]]

    stays = core == t // held

    sizes = [nev // 8 * n for n in EIGHTHS]
    begins = [sum(sizes[:n]) for n in range(len(sizes))]

    def send(e, h, after):
        line = (e + t) % held * nev + begins[h]
        piece = lax.dynamic_slice(after, (0, line, 0), (2, sizes[h], after.shape[2]))
        return move(piece, route(e))

    arrived = [[send(e, 0, sink) for e in range(held)]]

    sources = {}
    for name, r, part, parts in rounds(chips):
        q = pair_list[times * ((z + r) % chips) + t, 0]
        width = cols // parts
        piece = lax.dynamic_slice(source_elem, (0, 0, q * nev, part * width), (2, tsrc, nev, width))
        if r:
            piece = move(piece, along(r))
        sources[name] = (piece, move(piece, swap))

    other = move(mine, swap)
    where = jnp.stack([t, d]).astype(jnp.int32)
    made = spin_blocks(nev, tsrc, held, chips, where, pair_list, spin_sets, mine, other)
    info = jnp.stack([stays.astype(jnp.int32), t % held * nev]).astype(jnp.int32)
    mats = matrices(nev, tsrc, info, made, [move(made[e], route(e)) for e in range(held)])
    later, _ = lax.optimization_barrier((sink, mine))
    for h in range(1, len(sizes)):
        arrived.append([send(e, h, later) for e in range(held)])

    ys = []
    for h in range(len(sizes)):
        info = jnp.stack([stays.astype(jnp.int32), t % held * nev + begins[h]]).astype(jnp.int32)
        ys.append(modes(nev, tsrc, info, sink, arrived[h], mats, 48 if h < len(sizes) - 2 else 63))

    total = jnp.zeros((held * tsrc * 2, nev), jnp.float32)
    places = {}
    for name, r, part, parts in rounds(chips):
        came = (z - r) % chips
        places[name] = [
            ((came * CORES + side) * parts + part) * STEPS for side in (core, (core + 1) % CORES)
        ]
    for name, first, last, cuts, names in products(len(sizes), chips):
        total = inner_products(
            nev,
            tsrc,
            ys[first:last],
            begins[first],
            [cut - first for cut in cuts],
            [sources[n] for n in names],
            jnp.stack([at for n in names for at in places[n]]).astype(jnp.int32),
            mats,
            total,
            name == "last",
        )

    spread = jnp.broadcast_to(total[:1][None], (times * depth, 1, nev))
    spread = lax.all_to_all(spread, AXES, 0, 0, tiled=True)
    values = spread[:, 0, : held * tsrc * 2].reshape(times, chips, CORES, held, tsrc, 2)
    slot_of = (jnp.arange(times) - t) % held
    pick = (jnp.arange(held)[None, None] == slot_of[:, None, None]) & (
        jnp.arange(CORES)[None, :, None] == t // held
    )
    values = jnp.where(pick[:, None, :, :, None, None], values, 0.0)
    values = jnp.sum(values, axis=(2, 3)) * (1.0 / float(nev**3))
    values = jnp.transpose(values, (3, 2, 1, 0)).reshape(2, 1, tsrc, nop, 1)
    return values


def rounds(chips):
    half = chips // 2
    pieces = [(f"{r}", r, 0, 1) for r in range(half)]
    return pieces + [(f"{r}{'ab'[part]}", r, part, 2) for part in range(2) for r in range(half, chips)]


def products(chunks, chips):
    names = [name for name, *_ in rounds(chips)]
    late = chips - chips // 2
    soon, then, last = names[: chips // 2], names[chips // 2 : -late], names[-late:]
    return [
        ("early", 0, 2, [0] * len(soon), soon),
        ("next", 2, chunks - 2, [2] * len(soon), soon),
        ("middle", 0, chunks - 1, [chunks - 2] * len(soon) + [0] * len(then), soon + then),
        ("last", 0, chunks, [chunks - 1] * len(soon + then) + [0] * len(last), soon + then + last),
    ]


def solution(mesh):
    times, depth = mesh.shape["tm"], mesh.shape["op"]

    def on_device(sink_elem, source_elem, peram, pair_list, spin_sets):
        nop, pairs = pair_list.shape
        nev = source_elem.shape[2] // nop
        nspin = peram.shape[4] // nev
        tsrc = source_elem.shape[1]
        rows = sink_elem.shape[2]
        fits = (
            depth % CORES == 0
            and rows % nev == 0
            and rows // nev * CORES == times
            and sink_elem.shape[1] == 1
            and pairs == 1
            and nev % (8 * ROWS) == 0
            and nev % peram.shape[3] == 0
        )
        if fits:
            return chip_plan(nev, nop, tsrc, times, depth, sink_elem, source_elem, peram, pair_list, spin_sets)
        return baseline_plan(nev, nspin, nop, tsrc, pairs, sink_elem, source_elem, peram, pair_list, spin_sets)

    in_specs = (
        P(None, "tm", "op", None),
        P(None, None, None, "op"),
        P(None, "tm", None, "op", None),
        P(),
        P(),
    )
    out_specs = P(None, "tm", None, None, None)
    return jax.shard_map(on_device, mesh=mesh, in_specs=in_specs, out_specs=out_specs, check_vma=False)
```
